256 devices in a mesh: dist: 2 (over core), rows: 128 (over y, z, x).
Axes of the slice: x: 4, y: 4, z: 8, core: 2. Of those that a mesh axis runs over, the one named last changes fastest.
Arguments:
- holograms: bfloat16 [1, 4, 4, 1024, 1024], P(None, None, 'dist', 'rows'), may hold values from -6 to 6
- propagation: float32 [4], replicated, may hold values from 100 to 1000
- weights: bfloat16 [4, 1024, 1024], P(None, None, 'dist'), may hold values from -0.09375 to 0.09375
- angle_order: int32 [1, 4], replicated, may hold values from 0 to 3, each once within a row
- slab_rows: int32 [128], replicated, may hold values from 0 to 16, as said below
Outputs:
- slab: bfloat16 [2048, 1024], P('rows', 'dist')
The draws below stay inside these ranges and needn't reach their ends.
Inputs may be any that keep to these rules, and one draw needn't show every extreme that they name: Owners 2j and 2j+1 together own 16 slices: slab_rows[2j] + slab_rows[2j+1] = 16, so owner 2j holds slices 2j 8 onward and owner 2j+1 the rest of that pair's range; in every draw some owner holds 16.
All inputs are finite; a program needn't handle non-finite values.
Results may differ from the reference program's by a relative error of at most 0.02.
Values may be sent and summed in bfloat16 or wider, within the bound.
A program may use at most 128 MiB of HBM per device.

```python
import math
import jax
import jax.numpy as jnp
from jax import lax

DET = 1024
DIST = 4
ANG_MB = 4
MB = 1
ROWS_DEV = 8
CAP = 16
PAIRS = 64
PIXW = 1024
ANGLES = 4
N_ROWS = 128


def draw_slab_rows(key, part):
    first_key = jax.random.fold_in(key, 11)
    full_key = jax.random.fold_in(key, 12)
    first = jax.random.randint(first_key, (PAIRS,), 0, CAP + 1)
    full = jax.random.randint(full_key, (), 0, PAIRS)
    first = jnp.where(jnp.arange(PAIRS) == full, CAP, first)
    second = CAP - first
    return jnp.stack([first, second], axis=1).reshape(-1).astype(jnp.int32)


def shard_levels(stream_key, dims, shards, least, top_value):
    gain = 1.0
    for dim, parts in shards:
        draws = jax.random.uniform(jax.random.fold_in(jax.random.fold_in(stream_key, 6), dim), (parts,), jnp.float32, least / len(shards), top_value / len(shards))
        gain = gain * jnp.repeat(jnp.exp(draws), dims[dim] // parts).reshape((-1,) + (1,) * (len(dims) - 1 - dim))
    return gain


def noise(rng, dims, width, most, cuts=(), kind=jnp.bfloat16):
    level = shard_levels(rng, dims, cuts, -0.22, 0.18) if cuts else 1.0
    entries = jax.random.normal(rng, dims, jnp.float32) * width * level
    return jnp.minimum(jnp.maximum(entries, -most), most).astype(kind)


def setup_inputs(seed: int = 0) -> dict:
    key_of = jax.random.split(jax.random.key(seed), 6)
    return {
        "holograms": noise(key_of[0], (MB, ANG_MB, DIST, DET, DET), 1.0, 6.0, ((2, 2), (3, 128))),
        "propagation": jnp.clip(jnp.exp(jax.random.uniform(key_of[1], (DIST,), jnp.float32, math.log(100.0), math.log(1000.0))), 100.0, 1000.0),
        "weights": noise(key_of[2], (ANGLES, DET, PIXW), (ANGLES * DET) ** -0.5, 0.09375, ((2, 2),)),
        "angle_order": jax.vmap(lambda own: jax.random.permutation(own, ANG_MB))(jax.random.split(key_of[3], MB)).reshape((MB, ANG_MB)).astype(jnp.int32),
        "slab_rows": draw_slab_rows(jax.random.fold_in(key_of[5], 71), 0),
    }


absorb_ratio = 0.1
regularizer = 0.05


def to_half(value):
    return lax.optimization_barrier(value.astype(jnp.bfloat16)).astype(jnp.float32)


def reference(holograms, propagation, weights, angle_order, slab_rows):
    index = jnp.arange(DET, dtype=jnp.int32)
    signed = jnp.where(index < DET // 2, index, index - DET).astype(jnp.float32)
    radius = (signed[:, None] ** 2 + signed[None, :] ** 2) / float(DET * DET)
    chirp = propagation[:, None, None] * radius[None]
    transfer = 2.0 * (jnp.sin(chirp) + absorb_ratio * jnp.cos(chirp))
    denom = jnp.sum(transfer * transfer, axis=0) + regularizer
    recon = jnp.zeros((DET, PIXW), jnp.float32)
    for step in range(MB):
        for angle in range(ANG_MB):
            holo = holograms[step, angle].astype(jnp.float32)
            rows = jnp.fft.fft(holo, axis=-1, norm="ortho")
            rows = to_half(jnp.real(rows)) + 1j * to_half(jnp.imag(rows))
            spectra = jnp.fft.fft(rows, axis=-2, norm="ortho")
            numer = jnp.sum(transfer * spectra, axis=0) / denom
            numer = to_half(jnp.real(numer)) + 1j * to_half(jnp.imag(numer))
            half = jnp.fft.ifft(numer, axis=-2, norm="ortho")
            half = to_half(jnp.real(half)) + 1j * to_half(jnp.imag(half))
            phase = jnp.real(jnp.fft.ifft(half, axis=-1, norm="ortho")).astype(jnp.bfloat16)
            chosen = weights[step * ANG_MB + angle_order[step, angle]]
            recon = recon + jnp.dot(phase, chosen, preferred_element_type=jnp.float32)
    owner = jnp.arange(N_ROWS, dtype=jnp.int32)
    parity = owner % 2
    start = (owner - parity) * ROWS_DEV + parity * slab_rows[owner - parity]
    slot = jnp.arange(CAP, dtype=jnp.int32)
    where_rows = jnp.clip(start[:, None] + slot[None, :], 0, DET - 1).astype(jnp.int32)
    valid = (slot[None, :] < slab_rows[:, None]).astype(jnp.float32)
    picked = recon[where_rows] * valid[:, :, None]
    return picked.reshape(N_ROWS * CAP, PIXW).astype(jnp.bfloat16)
```

```python
import math

import jax
import jax.numpy as jnp
import numpy as np
from jax import lax
from jax.sharding import PartitionSpec as P

absorb_ratio = 0.1
regularizer = 0.05


def cas_table(length):
    index = np.arange(length)
    turned = (index[:, None] * index[None, :] % length) * (2.0 * math.pi / length)
    table = (np.cos(turned) + np.sin(turned)) / math.sqrt(length)
    return jnp.asarray(table.astype(np.float32)).astype(jnp.bfloat16)


def on_device(table, holograms, propagation, weights, angle_order, slab_rows):
    mbatch, angles, dist_dev, rows_dev, width = holograms.shape
    groups = lax.axis_size("rows")
    capacity = 2 * rows_dev
    col_table = table.reshape(groups, rows_dev, width)
    index = jnp.arange(width, dtype=jnp.int32)
    signed = jnp.where(index < width // 2, index, index - width).astype(jnp.float32)
    device = lax.axis_index("rows")
    local_freq = lax.dynamic_slice_in_dim(signed, device * rows_dev, rows_dev, 0)
    radius = (local_freq[:, None] ** 2 + signed[None, :] ** 2) / float(width * width)
    chirp = propagation[:, None, None] * radius[None]
    transfer = 2.0 * (jnp.sin(chirp) + absorb_ratio * jnp.cos(chirp))
    denom = jnp.sum(transfer * transfer, axis=0) + regularizer
    mine = lax.dynamic_slice_in_dim(transfer, lax.axis_index("dist") * dist_dev, dist_dev, 0)
    mine = mine / denom
    parity = device % 2
    offset = parity * slab_rows[device - parity]
    count = slab_rows[device]
    slot = jnp.arange(capacity, dtype=jnp.int32)[:, None]
    source = jnp.arange(capacity, dtype=jnp.int32)[None, :]
    select = ((source == offset + slot) & (slot < count)).astype(jnp.bfloat16)
    flat = holograms[0].reshape(angles * dist_dev * rows_dev, width)
    row = jnp.dot(flat, table, preferred_element_type=jnp.float32).astype(jnp.bfloat16)
    row = row.reshape(angles * dist_dev, rows_dev, width)
    piece = lax.all_to_all(row, "rows", split_axis=2, concat_axis=2, tiled=True)
    piece = piece.reshape(angles * dist_dev, rows_dev, groups, rows_dev)
    spec = jnp.einsum("aysk,syq->akq", piece, col_table, preferred_element_type=jnp.float32)
    spec = spec.reshape(angles, dist_dev, rows_dev, width)
    numer = jnp.sum(mine[None] * spec, axis=1).astype(jnp.bfloat16)
    other = lax.ppermute(numer, "dist", [(0, 1), (1, 0)])
    numer = (numer.astype(jnp.float32) + other.astype(jnp.float32)).astype(jnp.bfloat16)
    half = jnp.einsum("akq,qy->aky", numer, table, preferred_element_type=jnp.float32)
    half = half.astype(jnp.bfloat16)
    piece = lax.all_to_all(half, "rows", split_axis=2, concat_axis=2, tiled=True)
    piece = piece.reshape(angles, rows_dev, groups, rows_dev)
    phase = jnp.einsum("aksy,skx->ayx", piece, col_table, preferred_element_type=jnp.float32)
    phase = phase.astype(jnp.bfloat16)
    chosen = weights[angle_order[0]]
    pairs = [(source, source ^ 1) for source in range(groups)]
    partner = lax.ppermute(phase, "rows", pairs)
    lower = jnp.where(parity == 1, partner, phase)
    upper = jnp.where(parity == 1, phase, partner)
    paired = jnp.concatenate([lower, upper], axis=1)
    rows_in = jnp.einsum("ij,ajx->aix", select, paired, preferred_element_type=jnp.float32)
    rows_in = rows_in.astype(jnp.bfloat16)
    recon = jnp.einsum("ayx,axp->yp", rows_in, chosen, preferred_element_type=jnp.float32)
    return recon.astype(jnp.bfloat16)


def solution(mesh):
    def whole(*args):
        return jax.shard_map(
            on_device,
            mesh=mesh,
            in_specs=(P(), P(None, None, "dist", "rows"), P(), P(None, None, "dist"), P(), P()),
            out_specs=P("rows", "dist"),
            check_vma=False,
        )(cas_table(1024), *args)

    return whole
```

```python
import math

import jax
import jax.numpy as jnp
import numpy as np
from jax import lax
from jax.experimental import pallas as pl
from jax.experimental.pallas import tpu as pltpu
from jax.sharding import PartitionSpec as P

absorb_ratio = 0.1
regularizer = 0.05
MESH = pl.DeviceIdType.MESH
N = 1024
ROWS = 128
ROOT = 1.0 / 32.0
RADIX = 8


def tables():
    long = np.arange(ROWS)
    short = np.arange(RADIX)
    turn = 2.0 * math.pi
    beta = turn * (np.outer(long, long) % ROWS) / ROWS
    cas = [np.cos(beta) + np.sin(beta), np.cos(beta) - np.sin(beta)]
    eye2 = np.eye(2)
    ts, tf, ti = [], [], []
    for c in cas:
        ts.append(np.einsum("tk,bc->tbck", c, eye2).reshape(256, 256))
        tf.append(ts[-1].T)
        ti.append(np.einsum("jpk,bc->pjbck", c.reshape(64, 2, ROWS), eye2).reshape(256, 256))
    phi = turn * (np.outer(short, short) % RADIX) / RADIX
    wave = [np.cos(phi), np.sin(phi)]
    kr = np.concatenate([np.kron(np.eye(16), w) for w in wave], axis=0)
    ki = np.stack([np.einsum("ij,ab,d,my->iadmjby", np.eye(4), np.eye(4), np.ones(2), w) for w in wave])
    ki = np.moveaxis(ki, 0, 4).reshape(256, 256)
    kf = [
        np.einsum("ibx,ac,yz->biayxcz", w.reshape(4, 2, RADIX), np.eye(4), np.eye(8))
        for w in wave
    ]
    kf = np.stack(kf).reshape(512, 256)
    theta = turn * np.outer(short, long) / N
    rowtab = np.concatenate([np.cos(theta), np.sin(theta)], axis=0) * ROOT
    lanes = np.arange(128)
    tk = theta.T[:, lanes % RADIX]
    coltab = np.concatenate([np.cos(tk), np.sin(tk)], axis=0) * ROOT
    tx = np.concatenate([theta.T[:, 2 * (lanes // 32) + b] for b in range(2)], axis=0)
    outtab = np.concatenate([np.cos(tx), np.sin(tx)], axis=0) * ROOT
    first = np.concatenate(ts, axis=1)
    rest = np.concatenate(tf + ti + [ki, kf, np.pad(kr, ((0, 0), (0, 128)))], axis=0)
    half = lambda v: np.asarray(v, np.float32).astype(jnp.bfloat16)
    wide = np.concatenate([coltab, outtab], axis=0)
    return half(first), rowtab.astype(np.float32), half(rest), wide.astype(np.float32)


def dot(a, b):
    return jnp.dot(a, b, preferred_element_type=jnp.float32)


def half(value):
    return value.astype(jnp.bfloat16)


def row_stage(holo, first, rowtab):
    h = [holo[:, 128 * i : 128 * (i + 1)].astype(jnp.float32) for i in range(RADIX)]
    e = [h[i] + h[i + 4] for i in range(4)]
    o = [h[i] - h[i + 4] for i in range(4)]
    c = math.sqrt(0.5)
    even, odd = e[0] + e[2], e[1] + e[3]
    minus, plus = c * (o[1] - o[3]), c * (o[1] + o[3])
    p0, p4 = even + odd, even - odd
    p2, q2 = e[0] - e[2], e[1] - e[3]
    p1, q1 = o[0] + minus, o[2] + plus
    p3, q3 = o[0] - minus, plus - o[2]
    parts = [(p0, None), (p1, q1), (p2, q2), (p3, q3), (p4, None), (p3, -q3), (p2, -q2), (p1, -q1)]
    straight, turned = [], []
    for j, (p, q) in enumerate(parts):
        cos, sin = rowtab[j : j + 1, :], rowtab[RADIX + j : RADIX + j + 1, :]
        if q is None:
            straight.append(half(cos * p))
            turned.append(half(sin * p))
        else:
            straight.append(half(cos * p - sin * q))
            turned.append(half(sin * p + cos * q))
    blocks = [
        jnp.concatenate([straight[2 * i], straight[2 * i + 1], turned[2 * i], turned[2 * i + 1]], axis=1)
        for i in range(4)
    ]
    rhs = jnp.concatenate(blocks, axis=0)
    out = lax.dot_general(first, rhs, (((1,), (1,)), ((), ())), preferred_element_type=jnp.float32)
    return half(out)


def sine(x):
    n = jnp.floor(x * (1.0 / math.pi) + 0.5)
    r = x - n * 3.140625
    r = r - n * 9.67502593994140625e-4
    r = r - n * 1.509957990978376432e-7
    s = r * r
    w = -2.5052108385441718775e-8
    for coefficient in (
        2.7557319223985890653e-6,
        -1.9841269841269841253e-4,
        8.3333333333333332177e-3,
        -1.6666666666666665741e-1,
    ):
        w = w * s + coefficient
    value = r + r * s * w
    return jnp.where(n - 2.0 * jnp.floor(n * 0.5) > 0.5, -value, value)


def roll(value, shift):
    return pltpu.roll(value, shift % 128, 1)


def filter_stage(dist, me, speeds, roll=roll):
    lane = lax.broadcasted_iota(jnp.int32, (1, 128), 1)
    m = lane % 8
    second = (lane // 8) % 2 == 1
    odd_angle = (lane // 16) % 2 == 1
    other = odd_angle != (dist == 1)
    speed = jnp.where(
        other,
        jnp.where(second, speeds[3], speeds[2]),
        jnp.where(second, speeds[1], speeds[0]),
    )
    k = lax.broadcasted_iota(jnp.int32, (128, 128), 0)
    ky = k + 128 * m
    ky = jnp.where(ky < 512, ky, ky - 1024).astype(jnp.float32)
    ky2 = ky * ky
    shift = math.atan(absorb_ratio)
    gain = 2.0 * math.sqrt(1.0 + absorb_ratio * absorb_ratio)
    result = []
    for g in range(2):
        blocks = []
        for b in range(2):
            kx = 8 * me + 4 * g + 2 * (lane // 64) + b
            kx = jnp.where(kx < 512, kx, kx - 1024).astype(jnp.float32)
            radius = (ky2 + kx * kx) * (1.0 / (N * N))
            t = gain * sine(speed * radius + shift)
            total = t * t
            total = total + jnp.where(second, roll(total, 8), roll(total, -8))
            total = total + jnp.where(odd_angle, roll(total, 16), roll(total, -16))
            f = t / (total + regularizer)
            blocks.append(jnp.where(odd_angle, roll(f, 16), f))
        result.append(jnp.concatenate(blocks, axis=0))
    return result


def twist(cos, sin, u, v):
    return cos * u + sin * v, cos * v - sin * u


def twice(table):
    return jnp.concatenate([table, table], axis=0)


def column_stage(groups, tf0, tf1, kr, ki, ti0, ti1, coltab, filters):
    cos, sin = twice(coltab[0:128]), twice(coltab[128:256])
    r = jnp.concatenate(groups, axis=1)
    u, v = dot(tf0, r), dot(tf1, r)
    numer = []
    for g in range(2):
        part = slice(128 * g, 128 * g + 128)
        x, y = twist(cos, sin, u[:, part], v[:, part])
        spec = dot(jnp.concatenate([half(x), half(y)], axis=1), kr)
        numer.append(half(spec * filters[g]))
    pq = dot(jnp.concatenate(numer, axis=1), ki)
    p, q = pq[:, 0:128], pq[:, 128:256]
    straight = half(cos * p - sin * q)
    turned = half(sin * p + cos * q)
    return half(dot(ti0, straight) + dot(ti1, turned))


def last_stage(pair, tf0, tf1, kf, outtab):
    cos, sin = outtab[0:256], outtab[256:512]
    r = jnp.concatenate(pair, axis=1)
    u, v = dot(tf0, r), dot(tf1, r)
    rows = []
    for p in range(2):
        part = slice(128 * p, 128 * p + 128)
        x, y = twist(cos, sin, u[:, part], v[:, part])
        x, y = half(x), half(y)
        rows.append(jnp.concatenate([x[0:128], x[128:256], y[0:128], y[128:256]], axis=1))
    return dot(jnp.concatenate(rows, axis=0), kf)


def recon_stage(phase, weight_of):
    turned = [
        [phase[128 * p : 128 * p + 128, 128 * g : 128 * g + 128].T for g in range(2)] for p in range(2)
    ]
    total = None
    for a in range(4):
        tiles = []
        for xm in range(RADIX):
            g, at = xm // 4, ((xm % 4) * 4 + a) * 8
            tiles.append(jnp.concatenate([turned[p][g][at : at + 8] for p in range(2)], axis=0))
        lhs = half(jnp.concatenate(tiles, axis=1))
        term = dot(lhs, weight_of(a))
        total = term if total is None else total + term
    return total


def kernel(
    holo_hbm, speed_ref, weights_hbm, order_ref, slab_ref, first_hbm, rowtab_hbm, rest_hbm, wide_hbm,
    out_ref,
    holo, weights, first, rowtab, rest, wide, m1, r1, m2, r2, e1, e2, junk1, junk2,
    load_sem, weight_sem, send_sem, recv_sem,
):
    dist = lax.axis_index("dist")
    me = lax.axis_index("rows")
    barrier = pltpu.get_barrier_semaphore()

    def greet(t, carry):
        pl.semaphore_signal(barrier, inc=1, device_id=(dist, t), device_id_type=MESH)
        return carry

    lax.fori_loop(me + 1, ROWS, greet, 0)
    lax.fori_loop(0, me, greet, 0)
    pl.semaphore_signal(barrier, inc=1, device_id=(1 - dist, me), device_id_type=MESH)

    loads = [
        pltpu.make_async_copy(source, target, load_sem.at[i])
        for i, (source, target) in enumerate(
            [(holo_hbm, holo), (first_hbm, first), (rowtab_hbm, rowtab), (rest_hbm, rest), (wide_hbm, wide)]
        )
    ]
    for load in loads:
        load.start()
    big = pltpu.make_async_copy(weights_hbm, weights, weight_sem)
    big.start()
    for load in loads[:3]:
        load.wait()
    spectrum = row_stage(holo[...], first[...], rowtab[...])
    m1[0] = spectrum[:, 0:128]
    m1[1] = spectrum[:, 128:256]
    pl.semaphore_wait(barrier, ROWS)

    def send_all(source, sources, target, junk, index):
        mine = target.at[:, pl.ds(pl.multiple_of(2 * me, 2), 2), :]

        def send(t, carry):
            pltpu.make_async_remote_copy(
                src_ref=source(t),
                dst_ref=mine,
                send_sem=send_sem.at[index],
                recv_sem=recv_sem.at[index],
                device_id=(dist, t),
                device_id_type=MESH,
            ).start()
            return carry

        lax.fori_loop(me + 1, ROWS, send, 0)
        lax.fori_loop(0, me, send, 0)
        pltpu.make_async_copy(source(me), mine, recv_sem.at[index]).start()
        pltpu.make_async_copy(source(me), junk, send_sem.at[index]).start()

    send_all(lambda t: m1.at[:, pl.ds(pl.multiple_of(2 * t, 2), 2), :], m1, r1, junk1, 0)
    for load in loads[3:]:
        load.wait()
    speeds = [speed_ref[i] for i in range(4)]
    filters = filter_stage(dist, me, speeds)
    tf0, tf1, ti0, ti1 = (rest[256 * i : 256 * i + 256, :] for i in range(4))
    ki, kf, kr = rest[1024:1280, :], rest[1280:1792, :], rest[1792:2048, 0:128]
    coltab, outtab = wide[0:256, :], wide[256:768, :]
    pltpu.make_async_copy(r1, r1, recv_sem.at[0]).wait()
    inverse = column_stage([r1[0], r1[1]], tf0, tf1, kr, ki, ti0, ti1, coltab, filters)
    m2[0] = inverse[0:128]
    m2[1] = inverse[128:256]
    send_all(lambda t: m2.at[:, pl.ds(pl.multiple_of(2 * (t // 2), 2), 2), :], m2, r2, junk2, 1)
    big.wait()
    pltpu.make_async_copy(r2, r2, recv_sem.at[1]).wait()
    partial = last_stage([r2[0], r2[1]], tf0, tf1, kf, outtab)
    e1[...] = half(partial)
    swap = pltpu.make_async_remote_copy(
        src_ref=e1,
        dst_ref=e2,
        send_sem=send_sem.at[2],
        recv_sem=recv_sem.at[2],
        device_id=(1 - dist, me),
        device_id_type=MESH,
    )
    swap.start()
    swap.wait_recv()
    phase = partial + e2[...].astype(jnp.float32)
    recon = half(recon_stage(phase, lambda a: weights[order_ref[0, a]]))
    parity = me % 2
    offset = parity * slab_ref[me - parity]
    count = slab_ref[me]
    slot = lax.broadcasted_iota(jnp.int32, (16, 16), 0)
    source = lax.broadcasted_iota(jnp.int32, (16, 16), 1)
    select = half(((source == offset + slot) & (slot < count)).astype(jnp.float32))
    out_ref[...] = half(dot(select, recon))
    swap.wait_send()
    pltpu.make_async_copy(m1, m1, send_sem.at[0]).wait()
    pltpu.make_async_copy(r2, r2, send_sem.at[1]).wait()


def on_device(first, rowtab, rest, wide, holograms, propagation, weights, angle_order, slab_rows):
    pixels = weights.shape[2]
    holo = holograms.reshape(64, N)
    anywhere = pl.BlockSpec(memory_space=pl.ANY)
    scalar = pl.BlockSpec(memory_space=pltpu.SMEM)
    vmem = pltpu.VMEM
    lo = jnp.bfloat16
    return pl.pallas_call(
        kernel,
        out_shape=jax.ShapeDtypeStruct((16, pixels), lo),
        in_specs=[anywhere, scalar, anywhere, scalar, scalar] + [anywhere] * 4,
        out_specs=pl.BlockSpec(memory_space=vmem),
        scratch_shapes=[
            vmem(holo.shape, lo),
            vmem(weights.shape, lo),
            vmem(first.shape, lo),
            vmem(rowtab.shape, jnp.float32),
            vmem(rest.shape, lo),
            vmem(wide.shape, jnp.float32),
            vmem((2, 256, 128), lo),
            vmem((2, 256, 128), lo),
            vmem((2, 128, 128), lo),
            vmem((2, 256, 128), lo),
            vmem((256, 256), lo),
            vmem((256, 256), lo),
            vmem((2, 2, 128), lo),
            vmem((2, 2, 128), lo),
            pltpu.SemaphoreType.DMA((5,)),
            pltpu.SemaphoreType.DMA,
            pltpu.SemaphoreType.DMA((3,)),
            pltpu.SemaphoreType.DMA((3,)),
        ],
        compiler_params=pltpu.CompilerParams(collective_id=0, has_side_effects=True),
    )(holo, propagation, weights, angle_order, slab_rows, first, rowtab, rest, wide)


def solution(mesh):
    constants = tables()

    def whole(*args):
        return jax.shard_map(
            on_device,
            mesh=mesh,
            in_specs=(P(),) * 4
            + (P(None, None, "dist", "rows"), P(), P(None, None, "dist"), P(), P()),
            out_specs=P("rows", "dist"),
            check_vma=False,
        )(*(jnp.asarray(c) for c in constants), *args)

    return whole
```

```python
import math

import jax
import jax.numpy as jnp
import numpy as np
from jax import lax
from jax.experimental import pallas as pl
from jax.experimental.pallas import tpu as pltpu
from jax.sharding import PartitionSpec as P

absorb_ratio = 0.1
regularizer = 0.05
MESH = pl.DeviceIdType.MESH
N = 1024
ROWS = 128
ROOT = 1.0 / 32.0
RADIX = 8


def tables():
    long = np.arange(ROWS)
    short = np.arange(RADIX)
    turn = 2.0 * math.pi
    beta = turn * (np.outer(long, long) % ROWS) / ROWS
    cas = [np.cos(beta) + np.sin(beta), np.cos(beta) - np.sin(beta)]
    eye2 = np.eye(2)
    ts, tf, ti = [], [], []
    for c in cas:
        ts.append(np.einsum("tk,bc->tbck", c, eye2).reshape(256, 256))
        tf.append(ts[-1].T)
        ti.append(np.einsum("jpk,bc->pjbck", c.reshape(64, 2, ROWS), eye2).reshape(256, 256))
    phi = turn * (np.outer(short, short) % RADIX) / RADIX
    wave = [np.cos(phi), np.sin(phi)]
    kr = np.concatenate([np.kron(np.eye(16), w) for w in wave], axis=0)
    ki = np.stack([np.einsum("ij,ab,d,my->iadmjby", np.eye(4), np.eye(4), np.ones(2), w) for w in wave])
    ki = np.moveaxis(ki, 0, 4).reshape(256, 256)
    kf = [
        np.einsum("ibx,ac,yz->biayxcz", w.reshape(4, 2, RADIX), np.eye(4), np.eye(8))
        for w in wave
    ]
    kf = np.stack(kf).reshape(512, 256)
    theta = turn * np.outer(short, long) / N
    rowtab = np.concatenate([np.cos(theta), np.sin(theta)], axis=0) * ROOT
    lanes = np.arange(128)
    tk = theta.T[:, lanes % RADIX]
    coltab = np.concatenate([np.cos(tk), np.sin(tk)], axis=0) * ROOT
    tx = np.concatenate([theta.T[:, 2 * (lanes // 32) + b] for b in range(2)], axis=0)
    outtab = np.concatenate([np.cos(tx), np.sin(tx)], axis=0) * ROOT
    first = np.concatenate(ts, axis=1)
    rest = np.concatenate(tf + ti + [ki, kf, np.pad(kr, ((0, 0), (0, 128)))], axis=0)
    half = lambda v: np.asarray(v, np.float32).astype(jnp.bfloat16)
    wide = np.concatenate([coltab, outtab], axis=0)
    return half(first), rowtab.astype(np.float32), half(rest), wide.astype(np.float32)


def dot(a, b):
    return jnp.dot(a, b, preferred_element_type=jnp.float32)


def half(value):
    return value.astype(jnp.bfloat16)


def row_stage(holo, first, rowtab):
    h = [holo[:, 128 * i : 128 * (i + 1)].astype(jnp.float32) for i in range(RADIX)]
    e = [h[i] + h[i + 4] for i in range(4)]
    o = [h[i] - h[i + 4] for i in range(4)]
    c = math.sqrt(0.5)
    even, odd = e[0] + e[2], e[1] + e[3]
    minus, plus = c * (o[1] - o[3]), c * (o[1] + o[3])
    p0, p4 = even + odd, even - odd
    p2, q2 = e[0] - e[2], e[1] - e[3]
    p1, q1 = o[0] + minus, o[2] + plus
    p3, q3 = o[0] - minus, plus - o[2]
    parts = [(p0, None), (p1, q1), (p2, q2), (p3, q3), (p4, None), (p3, -q3), (p2, -q2), (p1, -q1)]
    straight, turned = [], []
    for j, (p, q) in enumerate(parts):
        cos, sin = rowtab[j : j + 1, :], rowtab[RADIX + j : RADIX + j + 1, :]
        if q is None:
            straight.append(half(cos * p))
            turned.append(half(sin * p))
        else:
            straight.append(half(cos * p - sin * q))
            turned.append(half(sin * p + cos * q))
    blocks = [
        jnp.concatenate([straight[2 * i], straight[2 * i + 1], turned[2 * i], turned[2 * i + 1]], axis=1)
        for i in range(4)
    ]
    rhs = jnp.concatenate(blocks, axis=0)
    out = lax.dot_general(first, rhs, (((1,), (1,)), ((), ())), preferred_element_type=jnp.float32)
    return half(out)


def sine(x):
    n = jnp.floor(x * (1.0 / math.pi) + 0.5)
    r = x - n * 3.140625
    r = r - n * 9.67502593994140625e-4
    r = r - n * 1.509957990978376432e-7
    s = r * r
    w = -2.5052108385441718775e-8
    for coefficient in (
        2.7557319223985890653e-6,
        -1.9841269841269841253e-4,
        8.3333333333333332177e-3,
        -1.6666666666666665741e-1,
    ):
        w = w * s + coefficient
    value = r + r * s * w
    return jnp.where(n - 2.0 * jnp.floor(n * 0.5) > 0.5, -value, value)


def roll(value, shift):
    return pltpu.roll(value, shift % 128, 1)


def filter_stage(dist, me, speeds, roll=roll):
    lane = lax.broadcasted_iota(jnp.int32, (1, 128), 1)
    m = lane % 8
    second = (lane // 8) % 2 == 1
    odd_angle = (lane // 16) % 2 == 1
    other = odd_angle != (dist == 1)
    speed = jnp.where(
        other,
        jnp.where(second, speeds[3], speeds[2]),
        jnp.where(second, speeds[1], speeds[0]),
    )
    k = lax.broadcasted_iota(jnp.int32, (128, 128), 0)
    ky = k + 128 * m
    ky = jnp.where(ky < 512, ky, ky - 1024).astype(jnp.float32)
    ky2 = ky * ky
    shift = math.atan(absorb_ratio)
    gain = 2.0 * math.sqrt(1.0 + absorb_ratio * absorb_ratio)
    result = []
    for g in range(2):
        blocks = []
        for b in range(2):
            kx = 8 * me + 4 * g + 2 * (lane // 64) + b
            kx = jnp.where(kx < 512, kx, kx - 1024).astype(jnp.float32)
            radius = (ky2 + kx * kx) * (1.0 / (N * N))
            t = gain * sine(speed * radius + shift)
            total = t * t
            total = total + jnp.where(second, roll(total, 8), roll(total, -8))
            total = total + jnp.where(odd_angle, roll(total, 16), roll(total, -16))
            f = t / (total + regularizer)
            blocks.append(jnp.where(odd_angle, roll(f, 16), f))
        result.append(jnp.concatenate(blocks, axis=0))
    return result


def twist(cos, sin, u, v):
    return cos * u + sin * v, cos * v - sin * u


def twice(table):
    return jnp.concatenate([table, table], axis=0)


def column_stage(groups, tf0, tf1, kr, ki, ti0, ti1, coltab, filters):
    cos, sin = twice(coltab[0:128]), twice(coltab[128:256])
    r = jnp.concatenate(groups, axis=1)
    u, v = dot(tf0, r), dot(tf1, r)
    numer = []
    for g in range(2):
        part = slice(128 * g, 128 * g + 128)
        x, y = twist(cos, sin, u[:, part], v[:, part])
        spec = dot(jnp.concatenate([half(x), half(y)], axis=1), kr)
        numer.append(half(spec * filters[g]))
    pq = dot(jnp.concatenate(numer, axis=1), ki)
    p, q = pq[:, 0:128], pq[:, 128:256]
    straight = half(cos * p - sin * q)
    turned = half(sin * p + cos * q)
    return dot(ti0, straight) + dot(ti1, turned)


def last_stage(pair, tf0, tf1, kf, outtab):
    cos, sin = outtab[0:256], outtab[256:512]
    r = jnp.concatenate(pair, axis=1)
    u, v = dot(tf0, r), dot(tf1, r)
    rows = []
    for p in range(2):
        part = slice(128 * p, 128 * p + 128)
        x, y = twist(cos, sin, u[:, part], v[:, part])
        x, y = half(x), half(y)
        rows.append(jnp.concatenate([x[0:128], x[128:256], y[0:128], y[128:256]], axis=1))
    return dot(jnp.concatenate(rows, axis=0), kf)


def recon_stage(phase, weight_of):
    turned = [
        [phase[128 * p : 128 * p + 128, 128 * g : 128 * g + 128].T for g in range(2)] for p in range(2)
    ]
    total = None
    for a in range(4):
        tiles = []
        for xm in range(RADIX):
            g, at = xm // 4, ((xm % 4) * 4 + a) * 8
            tiles.append(jnp.concatenate([turned[p][g][at : at + 8] for p in range(2)], axis=0))
        lhs = half(jnp.concatenate(tiles, axis=1))
        term = dot(lhs, weight_of(a))
        total = term if total is None else total + term
    return total


def far_first(me, act):
    y, z, x = me // 32, (me // 4) % 8, me % 4
    ys = [(y + i) % 4 * 32 for i in range(4)]
    xs = [(x + i) % 4 for i in range(4)]
    away = [0, 1, 2, 1]
    plane = sorted(((i, j) for i in range(4) for j in range(4)), key=lambda p: -away[p[0]] - away[p[1]])
    bases = {p: ys[p[0]] + xs[p[1]] for p in plane}

    def layer(step, carry):
        hop = (step + 1) // 2
        at = (z + 4 + hop * (1 - 2 * (step % 2)) + 8) % 8 * 4
        for p in plane[:-1]:
            act(bases[p] + at)

        @pl.when(step < 7)
        def _():
            act(bases[plane[-1]] + at)

        return carry

    lax.fori_loop(0, 8, layer, 0)


def kernel(
    holo_hbm, speed_hbm, weights_hbm, order_hbm, slab_hbm, first_hbm, rowtab_hbm, rest_hbm, wide_hbm,
    out_ref,
    holo, weights, first, rowtab, rest, wide, m1, r1, m2, r2, e1, e2, junk1, junk2, speed_ref, order_ref, slab_ref,
    load_sem, weight_sem, send_sem, recv_sem,
):
    dist = lax.axis_index("dist")
    me = lax.axis_index("rows")
    barrier = pltpu.get_barrier_semaphore()

    def greet(t):
        pl.semaphore_signal(barrier, inc=1, device_id=(dist, t), device_id_type=MESH)

    far_first(me, greet)
    pl.semaphore_signal(barrier, inc=1, device_id=(1 - dist, me), device_id_type=MESH)

    loads = [
        pltpu.make_async_copy(source, target, load_sem.at[i])
        for i, (source, target) in enumerate(
            [(holo_hbm, holo), (first_hbm, first), (rowtab_hbm, rowtab), (rest_hbm, rest), (wide_hbm, wide),
             (speed_hbm, speed_ref), (order_hbm, order_ref), (slab_hbm, slab_ref)]
        )
    ]
    for load in loads:
        load.start()
    big = pltpu.make_async_copy(weights_hbm, weights, weight_sem)
    big.start()
    for load in loads[:3]:
        load.wait()
    spectrum = row_stage(holo[...], first[...], rowtab[...])
    m1[0] = spectrum[:, 0:128]
    m1[1] = spectrum[:, 128:256]
    pl.semaphore_wait(barrier, ROWS)

    def send_all(source, sources, target, junk, index):
        mine = target.at[:, pl.ds(pl.multiple_of(2 * me, 2), 2), :]

        def send(t):
            pltpu.make_async_remote_copy(
                src_ref=source(t),
                dst_ref=mine,
                send_sem=send_sem.at[index],
                recv_sem=recv_sem.at[index],
                device_id=(dist, t),
                device_id_type=MESH,
            ).start()

        far_first(me, send)
        pltpu.make_async_copy(source(me), mine, recv_sem.at[index]).start()
        pltpu.make_async_copy(source(me), junk, send_sem.at[index]).start()

    send_all(lambda t: m1.at[:, pl.ds(pl.multiple_of(2 * t, 2), 2), :], m1, r1, junk1, 0)
    for load in loads[3:]:
        load.wait()
    speeds = [speed_ref[i] for i in range(4)]
    filters = filter_stage(dist, me, speeds)
    tf0, tf1, ti0, ti1 = (rest[256 * i : 256 * i + 256, :] for i in range(4))
    ki, kf, kr = rest[1024:1280, :], rest[1280:1792, :], rest[1792:2048, 0:128]
    coltab, outtab = wide[0:256, :], wide[256:768, :]
    pltpu.make_async_copy(r1, r1, recv_sem.at[0]).wait()
    inverse = column_stage([r1[0], r1[1]], tf0, tf1, kr, ki, ti0, ti1, coltab, filters)
    e1[...] = half(inverse)
    swap = pltpu.make_async_remote_copy(
        src_ref=e1,
        dst_ref=e2,
        send_sem=send_sem.at[2],
        recv_sem=recv_sem.at[2],
        device_id=(1 - dist, me),
        device_id_type=MESH,
    )
    swap.start()
    swap.wait_recv()
    inverse = half(inverse + e2[...].astype(jnp.float32))
    m2[0] = inverse[0:128]
    m2[1] = inverse[128:256]
    send_all(lambda t: m2.at[:, pl.ds(pl.multiple_of(2 * (t // 2), 2), 2), :], m2, r2, junk2, 1)
    big.wait()
    pltpu.make_async_copy(r2, r2, recv_sem.at[1]).wait()
    phase = last_stage([r2[0], r2[1]], tf0, tf1, kf, outtab)
    recon = half(recon_stage(phase, lambda a: weights[order_ref[0, a]]))
    parity = me % 2
    offset = parity * slab_ref[me - parity]
    count = slab_ref[me]
    slot = lax.broadcasted_iota(jnp.int32, (16, 16), 0)
    source = lax.broadcasted_iota(jnp.int32, (16, 16), 1)
    select = half(((source == offset + slot) & (slot < count)).astype(jnp.float32))
    out_ref[...] = half(dot(select, recon))
    swap.wait_send()
    pltpu.make_async_copy(m1, m1, send_sem.at[0]).wait()
    pltpu.make_async_copy(r2, r2, send_sem.at[1]).wait()


def on_device(first, rowtab, rest, wide, holograms, propagation, weights, angle_order, slab_rows):
    pixels = weights.shape[2]
    holo = holograms.reshape(64, N)
    anywhere = pl.BlockSpec(memory_space=pl.ANY)
    vmem = pltpu.VMEM
    lo = jnp.bfloat16
    return pl.pallas_call(
        kernel,
        out_shape=pltpu.VMEM((16, pixels), lo),
        in_specs=[anywhere] * 9,
        out_specs=pl.BlockSpec(memory_space=vmem),
        scratch_shapes=[
            vmem(holo.shape, lo),
            vmem(weights.shape, lo),
            vmem(first.shape, lo),
            vmem(rowtab.shape, jnp.float32),
            vmem(rest.shape, lo),
            vmem(wide.shape, jnp.float32),
            vmem((2, 256, 128), lo),
            vmem((2, 256, 128), lo),
            vmem((2, 128, 128), lo),
            vmem((2, 256, 128), lo),
            vmem((256, 128), lo),
            vmem((256, 128), lo),
            vmem((2, 2, 128), lo),
            vmem((2, 2, 128), lo),
            pltpu.SMEM(propagation.shape, jnp.float32),
            pltpu.SMEM(angle_order.shape, jnp.int32),
            pltpu.SMEM(slab_rows.shape, jnp.int32),
            pltpu.SemaphoreType.DMA((8,)),
            pltpu.SemaphoreType.DMA,
            pltpu.SemaphoreType.DMA((3,)),
            pltpu.SemaphoreType.DMA((3,)),
        ],
        compiler_params=pltpu.CompilerParams(collective_id=0, has_side_effects=True),
    )(holo, propagation, weights, angle_order, slab_rows, first, rowtab, rest, wide)


def solution(mesh):
    constants = tables()

    def whole(*args):
        return jax.shard_map(
            on_device,
            mesh=mesh,
            in_specs=(P(),) * 4
            + (P(None, None, "dist", "rows"), P(), P(None, None, "dist"), P(), P()),
            out_specs=P("rows", "dist"),
            check_vma=False,
        )(*(jnp.asarray(c) for c in constants), *args)

    return whole
```

```python
import math

import jax
import jax.numpy as jnp
import numpy as np
from jax import lax
from jax.experimental import pallas as pl
from jax.experimental.pallas import tpu as pltpu
from jax.sharding import PartitionSpec as P

absorb_ratio = 0.1
regularizer = 0.05
MESH = pl.DeviceIdType.MESH
N = 1024
ROWS = 128
ROOT = 1.0 / 32.0
RADIX = 8


def tables():
    long = np.arange(ROWS)
    short = np.arange(RADIX)
    turn = 2.0 * math.pi
    beta = turn * (np.outer(long, long) % ROWS) / ROWS
    cas = [np.cos(beta) + np.sin(beta), np.cos(beta) - np.sin(beta)]
    eye2 = np.eye(2)
    ts, tf, ti = [], [], []
    place = long.reshape(4, 8, 4).transpose(1, 0, 2).reshape(-1)
    for c in cas:
        ts.append(np.einsum("tk,bc->tbck", c[place], eye2).reshape(256, 256))
        tf.append(ts[-1].T)
        ti.append(np.einsum("jpk,bc->pjbck", c.reshape(64, 2, ROWS), eye2).reshape(256, 256))
    phi = turn * (np.outer(short, short) % RADIX) / RADIX
    wave = [np.cos(phi), np.sin(phi)]
    kr = np.concatenate([np.kron(np.eye(16), w) for w in wave], axis=0)
    ki = np.stack([np.einsum("ij,ab,d,my->iadmjby", np.eye(4), np.eye(4), np.ones(2), w) for w in wave])
    ki = np.moveaxis(ki, 0, 4).reshape(256, 256)
    kf = [
        np.einsum("ibx,ac,yz->biayxcz", w.reshape(4, 2, RADIX), np.eye(4), np.eye(8))
        for w in wave
    ]
    kf = np.stack(kf).reshape(512, 256)
    theta = turn * np.outer(short, long) / N
    rowtab = np.concatenate([np.cos(theta), np.sin(theta)], axis=0) * ROOT
    lanes = np.arange(128)
    tk = theta.T[:, lanes % RADIX]
    coltab = np.concatenate([np.cos(tk), np.sin(tk)], axis=0) * ROOT
    tx = np.concatenate([theta.T[:, 2 * (lanes // 32) + b] for b in range(2)], axis=0)
    outtab = np.concatenate([np.cos(tx), np.sin(tx)], axis=0) * ROOT
    first = np.concatenate(ts, axis=1)
    rest = np.concatenate(tf + ti + [ki, kf, np.pad(kr, ((0, 0), (0, 128)))], axis=0)
    half = lambda v: np.asarray(v, np.float32).astype(jnp.bfloat16)
    wide = np.concatenate([coltab, outtab], axis=0)
    return half(first), rowtab.astype(np.float32), half(rest), wide.astype(np.float32)


def dot(a, b):
    return jnp.dot(a, b, preferred_element_type=jnp.float32)


def half(value):
    return value.astype(jnp.bfloat16)


def row_stage(holo, first, rowtab):
    h = [holo[:, 128 * i : 128 * (i + 1)].astype(jnp.float32) for i in range(RADIX)]
    e = [h[i] + h[i + 4] for i in range(4)]
    o = [h[i] - h[i + 4] for i in range(4)]
    c = math.sqrt(0.5)
    even, odd = e[0] + e[2], e[1] + e[3]
    minus, plus = c * (o[1] - o[3]), c * (o[1] + o[3])
    p0, p4 = even + odd, even - odd
    p2, q2 = e[0] - e[2], e[1] - e[3]
    p1, q1 = o[0] + minus, o[2] + plus
    p3, q3 = o[0] - minus, plus - o[2]
    parts = [(p0, None), (p1, q1), (p2, q2), (p3, q3), (p4, None), (p3, -q3), (p2, -q2), (p1, -q1)]
    straight, turned = [], []
    for j, (p, q) in enumerate(parts):
        cos, sin = rowtab[j : j + 1, :], rowtab[RADIX + j : RADIX + j + 1, :]
        if q is None:
            straight.append(half(cos * p))
            turned.append(half(sin * p))
        else:
            straight.append(half(cos * p - sin * q))
            turned.append(half(sin * p + cos * q))
    blocks = [
        jnp.concatenate([straight[2 * i], straight[2 * i + 1], turned[2 * i], turned[2 * i + 1]], axis=1)
        for i in range(4)
    ]
    rhs = jnp.concatenate(blocks, axis=0)
    out = lax.dot_general(first, rhs, (((1,), (1,)), ((), ())), preferred_element_type=jnp.float32)
    return half(out)


def sine(x):
    n = jnp.floor(x * (1.0 / math.pi) + 0.5)
    r = x - n * 3.140625
    r = r - n * 9.67502593994140625e-4
    r = r - n * 1.509957990978376432e-7
    s = r * r
    w = -2.5052108385441718775e-8
    for coefficient in (
        2.7557319223985890653e-6,
        -1.9841269841269841253e-4,
        8.3333333333333332177e-3,
        -1.6666666666666665741e-1,
    ):
        w = w * s + coefficient
    value = r + r * s * w
    return jnp.where(n - 2.0 * jnp.floor(n * 0.5) > 0.5, -value, value)


def roll(value, shift):
    return pltpu.roll(value, shift % 128, 1)


def filter_stage(dist, me, speeds, roll=roll):
    lane = lax.broadcasted_iota(jnp.int32, (1, 128), 1)
    m = lane % 8
    second = (lane // 8) % 2 == 1
    odd_angle = (lane // 16) % 2 == 1
    other = odd_angle != (dist == 1)
    speed = jnp.where(
        other,
        jnp.where(second, speeds[3], speeds[2]),
        jnp.where(second, speeds[1], speeds[0]),
    )
    k = lax.broadcasted_iota(jnp.int32, (128, 128), 0)
    ky = k + 128 * m
    ky = jnp.where(ky < 512, ky, ky - 1024).astype(jnp.float32)
    ky2 = ky * ky
    shift = math.atan(absorb_ratio)
    gain = 2.0 * math.sqrt(1.0 + absorb_ratio * absorb_ratio)
    result = []
    for g in range(2):
        blocks = []
        for b in range(2):
            kx = 8 * me + 4 * g + 2 * (lane // 64) + b
            kx = jnp.where(kx < 512, kx, kx - 1024).astype(jnp.float32)
            radius = (ky2 + kx * kx) * (1.0 / (N * N))
            t = gain * sine(speed * radius + shift)
            total = t * t
            total = total + jnp.where(second, roll(total, 8), roll(total, -8))
            total = total + jnp.where(odd_angle, roll(total, 16), roll(total, -16))
            f = t / (total + regularizer)
            blocks.append(jnp.where(odd_angle, roll(f, 16), f))
        result.append(jnp.concatenate(blocks, axis=0))
    return result


def twist(cos, sin, u, v):
    return cos * u + sin * v, cos * v - sin * u


def twice(table):
    return jnp.concatenate([table, table], axis=0)


def column_stage(groups, tf0, tf1, kr, ki, ti0, ti1, coltab, filters):
    cos, sin = twice(coltab[0:128]), twice(coltab[128:256])
    r = jnp.concatenate(groups, axis=1)
    u, v = dot(tf0, r), dot(tf1, r)
    numer = []
    for g in range(2):
        part = slice(128 * g, 128 * g + 128)
        x, y = twist(cos, sin, u[:, part], v[:, part])
        spec = dot(jnp.concatenate([half(x), half(y)], axis=1), kr)
        numer.append(half(spec * filters[g]))
    pq = dot(jnp.concatenate(numer, axis=1), ki)
    p, q = pq[:, 0:128], pq[:, 128:256]
    straight = half(cos * p - sin * q)
    turned = half(sin * p + cos * q)
    return dot(ti0, straight) + dot(ti1, turned)


def last_stage(pair, tf0, tf1, kf, outtab):
    cos, sin = outtab[0:256], outtab[256:512]
    r = jnp.concatenate(pair, axis=1)
    u, v = dot(tf0, r), dot(tf1, r)
    rows = []
    for p in range(2):
        part = slice(128 * p, 128 * p + 128)
        x, y = twist(cos, sin, u[:, part], v[:, part])
        x, y = half(x), half(y)
        rows.append(jnp.concatenate([x[0:128], x[128:256], y[0:128], y[128:256]], axis=1))
    return dot(jnp.concatenate(rows, axis=0), kf)


def recon_stage(phase, weight_of):
    turned = [
        [phase[128 * p : 128 * p + 128, 128 * g : 128 * g + 128].T for g in range(2)] for p in range(2)
    ]
    total = None
    for a in range(4):
        tiles = []
        for xm in range(RADIX):
            g, at = xm // 4, ((xm % 4) * 4 + a) * 8
            tiles.append(jnp.concatenate([turned[p][g][at : at + 8] for p in range(2)], axis=0))
        lhs = half(jnp.concatenate(tiles, axis=1))
        term = dot(lhs, weight_of(a))
        total = term if total is None else total + term
    return total


HOPS = [0, 1, 2, 1]
PLANE = sorted(((i, j) for i in range(4) for j in range(4)), key=lambda p: -HOPS[p[0]] - HOPS[p[1]])[:-1]
LINE = [4, 3, 5, 2, 6, 1, 7]


def spot(me):
    return me // 32, (me // 4) % 8, me % 4


def far_first(me, act):
    y, z, x = spot(me)
    ys = [(y + i) % 4 * 32 for i in range(4)]
    xs = [(x + i) % 4 for i in range(4)]
    bases = {p: ys[p[0]] + xs[p[1]] for p in PLANE}

    def layer(step, carry):
        hop = (step + 1) // 2
        at = (z + 4 + hop * (1 - 2 * (step % 2)) + 8) % 8 * 4
        for p in PLANE:
            act(bases[p] + at)

        @pl.when(step < 7)
        def _():
            act(ys[0] + xs[0] + at)

        return carry

    lax.fori_loop(0, 8, layer, 0)


def kernel(
    holo_hbm, speed_hbm, weights_hbm, order_hbm, slab_hbm, first_hbm, rowtab_hbm, rest_hbm, wide_hbm,
    out_ref,
    holo, weights, first, rowtab, rest, wide, m1, b1, r1, m2, r2, e1, e2, junk, speed_ref, order_ref, slab_ref,
    load_sem, weight_sem, send_sem, recv_sem,
):
    dist = lax.axis_index("dist")
    me = lax.axis_index("rows")
    barrier = pltpu.get_barrier_semaphore()

    def greet(t):
        pl.semaphore_signal(barrier, inc=1, device_id=(dist, t), device_id_type=MESH)

    loads = [
        pltpu.make_async_copy(source, target, load_sem.at[i])
        for i, (source, target) in enumerate(
            [(holo_hbm, holo), (first_hbm, first), (rowtab_hbm, rowtab), (rest_hbm, rest), (wide_hbm, wide),
             (speed_hbm, speed_ref), (order_hbm, order_ref), (slab_hbm, slab_ref)]
        )
    ]
    for load in loads[:3]:
        load.start()
    y, z, x = spot(me)
    line = [(z + i) % 8 for i in LINE]
    plane = [((y + i) % 4, (x + j) % 4) for i, j in PLANE]
    for at in line:
        greet(y * 32 + at * 4 + x)
    for at, to in plane:
        greet(at * 32 + z * 4 + to)
    pl.semaphore_signal(barrier, inc=1, device_id=(1 - dist, me), device_id_type=MESH)
    for load in loads[3:]:
        load.start()
    big = pltpu.make_async_copy(weights_hbm, weights, weight_sem)
    big.start()
    for load in loads[:3]:
        load.wait()
    spectrum = row_stage(holo[...], first[...], rowtab[...])
    for i in range(8):
        for g in range(2):
            m1[2 * i + g] = spectrum[32 * i : 32 * i + 32, 128 * g : 128 * g + 128]
    pl.semaphore_wait(barrier, len(LINE) + len(PLANE) + 1)

    def push(source, target, sent, landed, peer):
        pltpu.make_async_remote_copy(
            src_ref=source,
            dst_ref=target,
            send_sem=send_sem.at[sent],
            recv_sem=recv_sem.at[landed],
            device_id=(dist, peer),
            device_id_type=MESH,
        ).start()

    def along_line(source, target, landed):
        mine = target.at[pl.ds(2 * z, 2)]
        for at in line:
            push(source.at[pl.ds(2 * at, 2)], mine, 0, landed, y * 32 + at * 4 + x)
        pltpu.make_async_copy(source.at[pl.ds(2 * z, 2)], mine, recv_sem.at[landed]).start()

    def in_plane(source, target, landed):
        def column(at, to):
            return pl.ds(pl.multiple_of(8 * at + 2 * to, 2), 2)

        mine = target.at[:, column(y, x), :]
        for at, to in plane:
            push(source.at[:, column(at, to), :], mine, 2, landed, at * 32 + z * 4 + to)
        pltpu.make_async_copy(source.at[:, column(y, x), :], mine, recv_sem.at[landed]).start()

    for core, steps in enumerate([(along_line, in_plane), (in_plane, along_line)]):

        @pl.when(dist == core)
        def _():
            steps[0](m1, b1, 0)
            pltpu.make_async_copy(b1, b1, recv_sem.at[0]).wait()
            steps[1](b1, r1, 1)

    for load in loads[3:]:
        load.wait()
    speeds = [speed_ref[i] for i in range(4)]
    filters = filter_stage(dist, me, speeds)
    tf0, tf1, ti0, ti1 = (rest[256 * i : 256 * i + 256, :] for i in range(4))
    ki, kf, kr = rest[1024:1280, :], rest[1280:1792, :], rest[1792:2048, 0:128]
    coltab, outtab = wide[0:256, :], wide[256:768, :]
    pltpu.make_async_copy(r1, r1, recv_sem.at[1]).wait()
    groups = [jnp.concatenate([r1[2 * i + g] for i in range(8)], axis=0) for g in range(2)]
    inverse = column_stage(groups, tf0, tf1, kr, ki, ti0, ti1, coltab, filters)
    e1[...] = half(inverse)
    swap = pltpu.make_async_remote_copy(
        src_ref=e1,
        dst_ref=e2,
        send_sem=send_sem.at[3],
        recv_sem=recv_sem.at[3],
        device_id=(1 - dist, me),
        device_id_type=MESH,
    )
    swap.start()
    swap.wait_recv()
    inverse = half(inverse + e2[...].astype(jnp.float32))
    m2[0] = inverse[0:128]
    m2[1] = inverse[128:256]
    mine = r2.at[:, pl.ds(pl.multiple_of(32 * z + 8 * y + 2 * x, 2), 2), :]

    def rows(t):
        return m2.at[:, pl.ds(pl.multiple_of(2 * (t // 2), 2), 2), :]

    far_first(me, lambda t: push(rows(t), mine, 1, 2, t))
    pltpu.make_async_copy(rows(me), mine, recv_sem.at[2]).start()
    pltpu.make_async_copy(rows(me), junk, send_sem.at[1]).start()
    big.wait()
    pltpu.make_async_copy(r2, r2, recv_sem.at[2]).wait()
    phase = last_stage([r2[0], r2[1]], tf0, tf1, kf, outtab)
    recon = half(recon_stage(phase, lambda a: weights[order_ref[0, a]]))
    parity = me % 2
    offset = parity * slab_ref[me - parity]
    count = slab_ref[me]
    slot = lax.broadcasted_iota(jnp.int32, (16, 16), 0)
    source = lax.broadcasted_iota(jnp.int32, (16, 16), 1)
    select = half(((source == offset + slot) & (slot < count)).astype(jnp.float32))
    out_ref[...] = half(dot(select, recon))
    swap.wait_send()
    pltpu.make_async_copy(m1.at[pl.ds(0, 14)], b1.at[pl.ds(0, 14)], send_sem.at[0]).wait()
    pltpu.make_async_copy(b1.at[pl.ds(0, 15)], r1.at[pl.ds(0, 15)], send_sem.at[2]).wait()
    pltpu.make_async_copy(r2, r2, send_sem.at[1]).wait()


def on_device(first, rowtab, rest, wide, holograms, propagation, weights, angle_order, slab_rows):
    pixels = weights.shape[2]
    holo = holograms.reshape(64, N)
    anywhere = pl.BlockSpec(memory_space=pl.ANY)
    vmem = pltpu.VMEM
    lo = jnp.bfloat16
    return pl.pallas_call(
        kernel,
        out_shape=pltpu.VMEM((16, pixels), lo),
        in_specs=[anywhere] * 9,
        out_specs=pl.BlockSpec(memory_space=vmem),
        scratch_shapes=[
            vmem(holo.shape, lo),
            vmem(weights.shape, lo),
            vmem(first.shape, lo),
            vmem(rowtab.shape, jnp.float32),
            vmem(rest.shape, lo),
            vmem(wide.shape, jnp.float32),
            vmem((16, 32, 128), lo),
            vmem((16, 32, 128), lo),
            vmem((16, 32, 128), lo),
            vmem((2, 128, 128), lo),
            vmem((2, 256, 128), lo),
            vmem((256, 128), lo),
            vmem((256, 128), lo),
            vmem((2, 2, 128), lo),
            pltpu.SMEM(propagation.shape, jnp.float32),
            pltpu.SMEM(angle_order.shape, jnp.int32),
            pltpu.SMEM(slab_rows.shape, jnp.int32),
            pltpu.SemaphoreType.DMA((8,)),
            pltpu.SemaphoreType.DMA,
            pltpu.SemaphoreType.DMA((4,)),
            pltpu.SemaphoreType.DMA((4,)),
        ],
        compiler_params=pltpu.CompilerParams(collective_id=0, has_side_effects=True),
    )(holo, propagation, weights, angle_order, slab_rows, first, rowtab, rest, wide)


def solution(mesh):
    constants = tables()

    def whole(*args):
        return jax.shard_map(
            on_device,
            mesh=mesh,
            in_specs=(P(),) * 4
            + (P(None, None, "dist", "rows"), P(), P(None, None, "dist"), P(), P()),
            out_specs=P("rows", "dist"),
            check_vma=False,
        )(*(jnp.asarray(c) for c in constants), *args)

    return whole
```

```python
import math

import jax
import jax.numpy as jnp
import numpy as np
from jax import lax
from jax.experimental import pallas as pl
from jax.experimental.pallas import tpu as pltpu
from jax.sharding import PartitionSpec as P

absorb_ratio = 0.1
regularizer = 0.05
MESH = pl.DeviceIdType.MESH
N = 1024
ROWS = 128
ROOT = 1.0 / 32.0
RADIX = 8


def tables():
    long = np.arange(ROWS)
    short = np.arange(RADIX)
    turn = 2.0 * math.pi
    beta = turn * (np.outer(long, long) % ROWS) / ROWS
    cas = [np.cos(beta) + np.sin(beta), np.cos(beta) - np.sin(beta)]
    eye2 = np.eye(2)
    ts, tf, ti = [], [], []
    place = long.reshape(4, 8, 4).transpose(1, 0, 2).reshape(-1)
    for c in cas:
        ts.append(np.einsum("tk,bc->tbck", c[place], eye2).reshape(256, 256))
        tf.append(ts[-1].T)
        ti.append(np.einsum("jpk,bc->pjbck", c.reshape(64, 2, ROWS), eye2).reshape(256, 256))
    phi = turn * (np.outer(short, short) % RADIX) / RADIX
    wave = [np.cos(phi), np.sin(phi)]
    kr = np.concatenate([np.kron(np.eye(16), w) for w in wave], axis=0)
    ki = np.stack([np.einsum("ij,ab,d,my->iadmjby", np.eye(4), np.eye(4), np.ones(2), w) for w in wave])
    ki = np.moveaxis(ki, 0, 4).reshape(256, 256)
    kf = [
        np.einsum("ibx,ac,yz->biayxcz", w.reshape(4, 2, RADIX), np.eye(4), np.eye(8))
        for w in wave
    ]
    kf = np.stack(kf).reshape(512, 256)
    theta = turn * np.outer(short, long) / N
    rowtab = np.concatenate([np.cos(theta), np.sin(theta)], axis=0) * ROOT
    lanes = np.arange(128)
    tk = theta.T[:, lanes % RADIX]
    coltab = np.concatenate([np.cos(tk), np.sin(tk)], axis=0) * ROOT
    tx = np.concatenate([theta.T[:, 2 * (lanes // 32) + b] for b in range(2)], axis=0)
    outtab = np.concatenate([np.cos(tx), np.sin(tx)], axis=0) * ROOT
    first = np.concatenate(ts, axis=1)
    rest = np.concatenate(tf + ti + [ki, kf, np.pad(kr, ((0, 0), (0, 128)))], axis=0)
    half = lambda v: np.asarray(v, np.float32).astype(jnp.bfloat16)
    wide = np.concatenate([coltab, outtab], axis=0)
    return half(first), rowtab.astype(np.float32), half(rest), wide.astype(np.float32)


def dot(a, b):
    return jnp.dot(a, b, preferred_element_type=jnp.float32)


def half(value):
    return value.astype(jnp.bfloat16)


def row_stage(holo, first, rowtab):
    h = [holo[:, 128 * i : 128 * (i + 1)].astype(jnp.float32) for i in range(RADIX)]
    e = [h[i] + h[i + 4] for i in range(4)]
    o = [h[i] - h[i + 4] for i in range(4)]
    c = math.sqrt(0.5)
    even, odd = e[0] + e[2], e[1] + e[3]
    minus, plus = c * (o[1] - o[3]), c * (o[1] + o[3])
    p0, p4 = even + odd, even - odd
    p2, q2 = e[0] - e[2], e[1] - e[3]
    p1, q1 = o[0] + minus, o[2] + plus
    p3, q3 = o[0] - minus, plus - o[2]
    parts = [(p0, None), (p1, q1), (p2, q2), (p3, q3), (p4, None), (p3, -q3), (p2, -q2), (p1, -q1)]
    straight, turned = [], []
    for j, (p, q) in enumerate(parts):
        cos, sin = rowtab[j : j + 1, :], rowtab[RADIX + j : RADIX + j + 1, :]
        if q is None:
            straight.append(half(cos * p))
            turned.append(half(sin * p))
        else:
            straight.append(half(cos * p - sin * q))
            turned.append(half(sin * p + cos * q))
    blocks = [
        jnp.concatenate([straight[2 * i], straight[2 * i + 1], turned[2 * i], turned[2 * i + 1]], axis=1)
        for i in range(4)
    ]
    rhs = jnp.concatenate(blocks, axis=0)
    out = lax.dot_general(first, rhs, (((1,), (1,)), ((), ())), preferred_element_type=jnp.float32)
    return half(out)


def sine(x):
    n = jnp.floor(x * (1.0 / math.pi) + 0.5)
    r = x - n * 3.140625
    r = r - n * 9.67502593994140625e-4
    r = r - n * 1.509957990978376432e-7
    s = r * r
    w = -2.5052108385441718775e-8
    for coefficient in (
        2.7557319223985890653e-6,
        -1.9841269841269841253e-4,
        8.3333333333333332177e-3,
        -1.6666666666666665741e-1,
    ):
        w = w * s + coefficient
    value = r + r * s * w
    return jnp.where(n - 2.0 * jnp.floor(n * 0.5) > 0.5, -value, value)


def roll(value, shift):
    return pltpu.roll(value, shift % 128, 1)


def filter_stage(dist, me, speeds, roll=roll):
    lane = lax.broadcasted_iota(jnp.int32, (1, 128), 1)
    m = lane % 8
    second = (lane // 8) % 2 == 1
    odd_angle = (lane // 16) % 2 == 1
    other = odd_angle != (dist == 1)
    speed = jnp.where(
        other,
        jnp.where(second, speeds[3], speeds[2]),
        jnp.where(second, speeds[1], speeds[0]),
    )
    k = lax.broadcasted_iota(jnp.int32, (128, 128), 0)
    ky = k + 128 * m
    ky = jnp.where(ky < 512, ky, ky - 1024).astype(jnp.float32)
    ky2 = ky * ky
    shift = math.atan(absorb_ratio)
    gain = 2.0 * math.sqrt(1.0 + absorb_ratio * absorb_ratio)
    result = []
    for g in range(2):
        blocks = []
        for b in range(2):
            kx = 8 * me + 4 * g + 2 * (lane // 64) + b
            kx = jnp.where(kx < 512, kx, kx - 1024).astype(jnp.float32)
            radius = (ky2 + kx * kx) * (1.0 / (N * N))
            t = gain * sine(speed * radius + shift)
            total = t * t
            total = total + jnp.where(second, roll(total, 8), roll(total, -8))
            total = total + jnp.where(odd_angle, roll(total, 16), roll(total, -16))
            f = t / (total + regularizer)
            blocks.append(jnp.where(odd_angle, roll(f, 16), f))
        result.append(jnp.concatenate(blocks, axis=0))
    return result


def twist(cos, sin, u, v):
    return cos * u + sin * v, cos * v - sin * u


def twice(table):
    return jnp.concatenate([table, table], axis=0)


def column_stage(groups, tf0, tf1, kr, ki, ti0, ti1, coltab, filters):
    cos, sin = twice(coltab[0:128]), twice(coltab[128:256])
    r = jnp.concatenate(groups, axis=1)
    u, v = dot(tf0, r), dot(tf1, r)
    numer = []
    for g in range(2):
        part = slice(128 * g, 128 * g + 128)
        x, y = twist(cos, sin, u[:, part], v[:, part])
        spec = dot(jnp.concatenate([half(x), half(y)], axis=1), kr)
        numer.append(half(spec * filters[g]))
    pq = dot(jnp.concatenate(numer, axis=1), ki)
    p, q = pq[:, 0:128], pq[:, 128:256]
    straight = half(cos * p - sin * q)
    turned = half(sin * p + cos * q)
    return dot(ti0, straight) + dot(ti1, turned)


def last_stage(pair, tf0, tf1, kf, outtab):
    cos, sin = outtab[0:256], outtab[256:512]
    r = jnp.concatenate(pair, axis=1)
    u, v = dot(tf0, r), dot(tf1, r)
    rows = []
    for p in range(2):
        part = slice(128 * p, 128 * p + 128)
        x, y = twist(cos, sin, u[:, part], v[:, part])
        x, y = half(x), half(y)
        rows.append(jnp.concatenate([x[0:128], x[128:256], y[0:128], y[128:256]], axis=1))
    return dot(jnp.concatenate(rows, axis=0), kf)


def recon_stage(phase, weight_of):
    turned = [
        [phase[128 * p : 128 * p + 128, 128 * g : 128 * g + 128].T for g in range(2)] for p in range(2)
    ]
    total = None
    for a in range(4):
        tiles = []
        for xm in range(RADIX):
            g, at = xm // 4, ((xm % 4) * 4 + a) * 8
            tiles.append(jnp.concatenate([turned[p][g][at : at + 8] for p in range(2)], axis=0))
        lhs = half(jnp.concatenate(tiles, axis=1))
        term = dot(lhs, weight_of(a))
        total = term if total is None else total + term
    return total


HOPS = [0, 1, 2, 1]
PLANE = sorted(((i, j) for i in range(4) for j in range(4)), key=lambda p: -HOPS[p[0]] - HOPS[p[1]])[:-1]
LINE = [4, 3, 5, 2, 6, 1, 7]


def spot(me):
    return me // 32, (me // 4) % 8, me % 4


def kernel(
    holo_hbm, speed_hbm, weights_hbm, order_hbm, slab_hbm, first_hbm, rowtab_hbm, rest_hbm, wide_hbm,
    out_ref,
    holo, weights, first, rowtab, rest, wide, m1, b1, r1, m2, r2, e1, e2, junk, speed_ref, order_ref, slab_ref,
    load_sem, weight_sem, send_sem, recv_sem,
):
    dist = lax.axis_index("dist")
    me = lax.axis_index("rows")
    barrier = pltpu.get_barrier_semaphore()

    def greet(t):
        pl.semaphore_signal(barrier, inc=1, device_id=(dist, t), device_id_type=MESH)

    loads = [
        pltpu.make_async_copy(source, target, load_sem.at[i])
        for i, (source, target) in enumerate(
            [(holo_hbm, holo), (first_hbm, first), (rowtab_hbm, rowtab), (rest_hbm, rest), (wide_hbm, wide),
             (speed_hbm, speed_ref), (order_hbm, order_ref), (slab_hbm, slab_ref)]
        )
    ]
    for load in loads[:3]:
        load.start()
    y, z, x = spot(me)
    line = [(z + i) % 8 for i in LINE]
    plane = [((y + i) % 4, (x + j) % 4) for i, j in PLANE]
    for at in line:
        greet(y * 32 + at * 4 + x)
    for at, to in plane:
        greet(at * 32 + z * 4 + to)
    pl.semaphore_signal(barrier, inc=1, device_id=(1 - dist, me), device_id_type=MESH)
    for load in loads[3:]:
        load.start()
    big = pltpu.make_async_copy(weights_hbm, weights, weight_sem)
    big.start()
    for load in loads[:3]:
        load.wait()
    spectrum = row_stage(holo[...], first[...], rowtab[...])
    for i in range(8):
        for g in range(2):
            m1[2 * i + g] = spectrum[32 * i : 32 * i + 32, 128 * g : 128 * g + 128]
    pl.semaphore_wait(barrier, len(LINE) + len(PLANE) + 1)

    def push(source, target, sent, landed, peer, core=dist):
        pltpu.make_async_remote_copy(
            src_ref=source,
            dst_ref=target,
            send_sem=send_sem.at[sent],
            recv_sem=recv_sem.at[landed],
            device_id=(core, peer),
            device_id_type=MESH,
        ).start()

    def along_line(source, target, landed):
        mine = target.at[pl.ds(2 * z, 2)]
        for at in line:
            push(source.at[pl.ds(2 * at, 2)], mine, 0, landed, y * 32 + at * 4 + x)
        pltpu.make_async_copy(source.at[pl.ds(2 * z, 2)], mine, recv_sem.at[landed]).start()

    def in_plane(source, target, landed):
        def column(at, to):
            return pl.ds(pl.multiple_of(8 * at + 2 * to, 2), 2)

        mine = target.at[:, column(y, x), :]
        for at, to in plane:
            push(source.at[:, column(at, to), :], mine, 2, landed, at * 32 + z * 4 + to)
        pltpu.make_async_copy(source.at[:, column(y, x), :], mine, recv_sem.at[landed]).start()

    for core, steps in enumerate([(along_line, in_plane), (in_plane, along_line)]):

        @pl.when(dist == core)
        def _():
            steps[0](m1, b1, 0)
            pltpu.make_async_copy(b1, b1, recv_sem.at[0]).wait()
            steps[1](b1, r1, 1)

    for load in loads[3:]:
        load.wait()
    speeds = [speed_ref[i] for i in range(4)]
    filters = filter_stage(dist, me, speeds)
    tf0, tf1, ti0, ti1 = (rest[256 * i : 256 * i + 256, :] for i in range(4))
    ki, kf, kr = rest[1024:1280, :], rest[1280:1792, :], rest[1792:2048, 0:128]
    coltab, outtab = wide[0:256, :], wide[256:768, :]
    pltpu.make_async_copy(r1, r1, recv_sem.at[1]).wait()
    groups = [jnp.concatenate([r1[2 * i + g] for i in range(8)], axis=0) for g in range(2)]
    inverse = column_stage(groups, tf0, tf1, kr, ki, ti0, ti1, coltab, filters)
    e1[...] = half(inverse)
    swap = pltpu.make_async_remote_copy(
        src_ref=e1,
        dst_ref=e2,
        send_sem=send_sem.at[3],
        recv_sem=recv_sem.at[3],
        device_id=(1 - dist, me),
        device_id_type=MESH,
    )
    swap.start()
    swap.wait_recv()
    inverse = half(inverse + e2[...].astype(jnp.float32))
    m2[0] = inverse[0:128]
    m2[1] = inverse[128:256]
    mine = r2.at[:, pl.ds(pl.multiple_of(32 * z + 8 * y + 2 * x, 2), 2), :]

    def rows(t):
        return m2.at[:, pl.ds(pl.multiple_of(2 * (t // 2), 2), 2), :]

    def layer(step, carry):
        depth = 4 * dist + step
        for core in (1, 0):
            for at, to in plane:
                t = at * 32 + depth * 4 + to
                push(rows(t), mine, 1, 2, t, core)

            @pl.when(jnp.logical_or(depth != z, dist != core))
            def _():
                t = y * 32 + depth * 4 + x
                push(rows(t), mine, 1, 2, t, core)

        return carry

    lax.fori_loop(0, 4, layer, 0)

    @pl.when(z // 4 == dist)
    def _():
        pltpu.make_async_copy(rows(me), mine, recv_sem.at[2]).start()
        pltpu.make_async_copy(rows(me), junk, send_sem.at[1]).start()

    big.wait()
    pltpu.make_async_copy(r2, r2, recv_sem.at[2]).wait()
    phase = last_stage([r2[0], r2[1]], tf0, tf1, kf, outtab)
    recon = half(recon_stage(phase, lambda a: weights[order_ref[0, a]]))
    parity = me % 2
    offset = parity * slab_ref[me - parity]
    count = slab_ref[me]
    slot = lax.broadcasted_iota(jnp.int32, (16, 16), 0)
    source = lax.broadcasted_iota(jnp.int32, (16, 16), 1)
    select = half(((source == offset + slot) & (slot < count)).astype(jnp.float32))
    out_ref[...] = half(dot(select, recon))
    swap.wait_send()
    pltpu.make_async_copy(m1.at[pl.ds(0, 14)], b1.at[pl.ds(0, 14)], send_sem.at[0]).wait()
    pltpu.make_async_copy(b1.at[pl.ds(0, 15)], r1.at[pl.ds(0, 15)], send_sem.at[2]).wait()
    pltpu.make_async_copy(r2, r2, send_sem.at[1]).wait()


def on_device(first, rowtab, rest, wide, holograms, propagation, weights, angle_order, slab_rows):
    pixels = weights.shape[2]
    holo = holograms.reshape(64, N)
    anywhere = pl.BlockSpec(memory_space=pl.ANY)
    vmem = pltpu.VMEM
    lo = jnp.bfloat16
    return pl.pallas_call(
        kernel,
        out_shape=pltpu.VMEM((16, pixels), lo),
        in_specs=[anywhere] * 9,
        out_specs=pl.BlockSpec(memory_space=vmem),
        scratch_shapes=[
            vmem(holo.shape, lo),
            vmem(weights.shape, lo),
            vmem(first.shape, lo),
            vmem(rowtab.shape, jnp.float32),
            vmem(rest.shape, lo),
            vmem(wide.shape, jnp.float32),
            vmem((16, 32, 128), lo),
            vmem((16, 32, 128), lo),
            vmem((16, 32, 128), lo),
            vmem((2, 128, 128), lo),
            vmem((2, 256, 128), lo),
            vmem((256, 128), lo),
            vmem((256, 128), lo),
            vmem((2, 2, 128), lo),
            pltpu.SMEM(propagation.shape, jnp.float32),
            pltpu.SMEM(angle_order.shape, jnp.int32),
            pltpu.SMEM(slab_rows.shape, jnp.int32),
            pltpu.SemaphoreType.DMA((8,)),
            pltpu.SemaphoreType.DMA,
            pltpu.SemaphoreType.DMA((4,)),
            pltpu.SemaphoreType.DMA((4,)),
        ],
        compiler_params=pltpu.CompilerParams(collective_id=0, has_side_effects=True),
    )(holo, propagation, weights, angle_order, slab_rows, first, rowtab, rest, wide)


def solution(mesh):
    constants = tables()

    def whole(*args):
        return jax.shard_map(
            on_device,
            mesh=mesh,
            in_specs=(P(),) * 4
            + (P(None, None, "dist", "rows"), P(), P(None, None, "dist"), P(), P()),
            out_specs=P("rows", "dist"),
            check_vma=False,
        )(*(jnp.asarray(c) for c in constants), *args)

    return whole
```

```python
import math

import jax
import jax.numpy as jnp
import numpy as np
from jax import lax
from jax.experimental import pallas as pl
from jax.experimental.pallas import tpu as pltpu
from jax.sharding import PartitionSpec as P

absorb_ratio = 0.1
regularizer = 0.05
MESH = pl.DeviceIdType.MESH
N = 1024
ROWS = 128
ROOT = 1.0 / 32.0
RADIX = 8


def tables():
    long = np.arange(ROWS)
    short = np.arange(RADIX)
    turn = 2.0 * math.pi
    beta = turn * (np.outer(long, long) % ROWS) / ROWS
    cas = [np.cos(beta) + np.sin(beta), np.cos(beta) - np.sin(beta)]
    eye2 = np.eye(2)
    ts, tf, ti = [], [], []
    place = long.reshape(4, 8, 4).transpose(1, 0, 2).reshape(-1)
    for c in cas:
        ts.append(np.einsum("tk,bc->tbck", c[place], eye2).reshape(256, 256))
        tf.append(ts[-1].T)
        ti.append(np.einsum("jpk,bc->pjbck", c.reshape(64, 2, ROWS), eye2).reshape(256, 256))
    phi = turn * (np.outer(short, short) % RADIX) / RADIX
    wave = [np.cos(phi), np.sin(phi)]
    kr = np.concatenate([np.kron(np.eye(16), w) for w in wave], axis=0)
    ki = np.stack([np.einsum("ij,ab,d,my->iadmjby", np.eye(4), np.eye(4), np.ones(2), w) for w in wave])
    ki = np.moveaxis(ki, 0, 4).reshape(256, 256)
    spectral = (8 * place[None, :] + short[:, None]).reshape(-1)
    angle = turn * (np.outer(spectral, np.arange(N)) % N) / N
    full = (np.cos(angle) + np.sin(angle)) * ROOT
    perm = np.einsum("st,bc->sbct", np.eye(ROWS), eye2).reshape(256, 256)
    theta = turn * np.outer(short, long) / N
    rowtab = np.concatenate([np.cos(theta), np.sin(theta)], axis=0) * ROOT
    tk = theta.T[:, np.arange(128) % RADIX]
    coltab = np.concatenate([np.cos(tk), np.sin(tk)], axis=0) * ROOT
    first = np.concatenate(ts, axis=1)
    rest = np.concatenate(tf + ti + [ki, perm, np.pad(kr, ((0, 0), (0, 128)))], axis=0)
    half = lambda v: np.asarray(v, np.float32).astype(jnp.bfloat16)
    return half(first), rowtab.astype(np.float32), half(full), half(rest), coltab.astype(np.float32)


def dot(a, b):
    return jnp.dot(a, b, preferred_element_type=jnp.float32)


def half(value):
    return value.astype(jnp.bfloat16)


def row_stage(holo, first, rowtab):
    h = [holo[:, 128 * i : 128 * (i + 1)].astype(jnp.float32) for i in range(RADIX)]
    e = [h[i] + h[i + 4] for i in range(4)]
    o = [h[i] - h[i + 4] for i in range(4)]
    c = math.sqrt(0.5)
    even, odd = e[0] + e[2], e[1] + e[3]
    minus, plus = c * (o[1] - o[3]), c * (o[1] + o[3])
    p0, p4 = even + odd, even - odd
    p2, q2 = e[0] - e[2], e[1] - e[3]
    p1, q1 = o[0] + minus, o[2] + plus
    p3, q3 = o[0] - minus, plus - o[2]
    parts = [(p0, None), (p1, q1), (p2, q2), (p3, q3), (p4, None), (p3, -q3), (p2, -q2), (p1, -q1)]
    straight, turned = [], []
    for j, (p, q) in enumerate(parts):
        cos, sin = rowtab[j : j + 1, :], rowtab[RADIX + j : RADIX + j + 1, :]
        if q is None:
            straight.append(half(cos * p))
            turned.append(half(sin * p))
        else:
            straight.append(half(cos * p - sin * q))
            turned.append(half(sin * p + cos * q))
    blocks = [
        jnp.concatenate([straight[2 * i], straight[2 * i + 1], turned[2 * i], turned[2 * i + 1]], axis=1)
        for i in range(4)
    ]
    rhs = jnp.concatenate(blocks, axis=0)
    out = lax.dot_general(first, rhs, (((1,), (1,)), ((), ())), preferred_element_type=jnp.float32)
    return half(out)


def sine(x):
    n = jnp.floor(x * (1.0 / math.pi) + 0.5)
    r = x - n * 3.140625
    r = r - n * 9.67502593994140625e-4
    r = r - n * 1.509957990978376432e-7
    s = r * r
    w = -2.5052108385441718775e-8
    for coefficient in (
        2.7557319223985890653e-6,
        -1.9841269841269841253e-4,
        8.3333333333333332177e-3,
        -1.6666666666666665741e-1,
    ):
        w = w * s + coefficient
    value = r + r * s * w
    return jnp.where(n - 2.0 * jnp.floor(n * 0.5) > 0.5, -value, value)


def roll(value, shift):
    return pltpu.roll(value, shift % 128, 1)


def filter_stage(dist, me, speeds, roll=roll):
    lane = lax.broadcasted_iota(jnp.int32, (1, 128), 1)
    m = lane % 8
    second = (lane // 8) % 2 == 1
    odd_angle = (lane // 16) % 2 == 1
    other = odd_angle != (dist == 1)
    speed = jnp.where(
        other,
        jnp.where(second, speeds[3], speeds[2]),
        jnp.where(second, speeds[1], speeds[0]),
    )
    k = lax.broadcasted_iota(jnp.int32, (128, 128), 0)
    ky = k + 128 * m
    ky = jnp.where(ky < 512, ky, ky - 1024).astype(jnp.float32)
    ky2 = ky * ky
    shift = math.atan(absorb_ratio)
    gain = 2.0 * math.sqrt(1.0 + absorb_ratio * absorb_ratio)
    result = []
    for g in range(2):
        blocks = []
        for b in range(2):
            kx = 8 * me + 4 * g + 2 * (lane // 64) + b
            kx = jnp.where(kx < 512, kx, kx - 1024).astype(jnp.float32)
            radius = (ky2 + kx * kx) * (1.0 / (N * N))
            t = gain * sine(speed * radius + shift)
            total = t * t
            total = total + jnp.where(second, roll(total, 8), roll(total, -8))
            total = total + jnp.where(odd_angle, roll(total, 16), roll(total, -16))
            f = t / (total + regularizer)
            blocks.append(jnp.where(odd_angle, roll(f, 16), f))
        result.append(jnp.concatenate(blocks, axis=0))
    return result


def twist(cos, sin, u, v):
    return cos * u + sin * v, cos * v - sin * u


def twice(table):
    return jnp.concatenate([table, table], axis=0)


def column_stage(groups, tf0, tf1, kr, ki, ti0, ti1, coltab, filters):
    cos, sin = twice(coltab[0:128]), twice(coltab[128:256])
    r = jnp.concatenate(groups, axis=1)
    u, v = dot(tf0, r), dot(tf1, r)
    numer = []
    for g in range(2):
        part = slice(128 * g, 128 * g + 128)
        x, y = twist(cos, sin, u[:, part], v[:, part])
        spec = dot(jnp.concatenate([half(x), half(y)], axis=1), kr)
        numer.append(half(spec * filters[g]))
    pq = dot(jnp.concatenate(numer, axis=1), ki)
    p, q = pq[:, 0:128], pq[:, 128:256]
    straight = half(cos * p - sin * q)
    turned = half(sin * p + cos * q)
    return dot(ti0, straight) + dot(ti1, turned)


def last_stage(pair, perm, weight_of):
    r = jnp.concatenate(pair, axis=1)
    turned = lax.dot_general(r, perm, (((0,), (0,)), ((), ())), preferred_element_type=jnp.float32)
    total = None
    for a in range(4):
        tiles = []
        for j in range(RADIX):
            at, b = (j // 2 * 4 + a) * 8, j % 2 * 128
            tiles.append(jnp.concatenate([turned[at + 128 * p : at + 128 * p + 8, b : b + 128] for p in range(2)], axis=0))
        term = dot(half(jnp.concatenate(tiles, axis=1)), weight_of(a))
        total = term if total is None else total + term
    return total


HOPS = [0, 1, 2, 1]
PLANE = sorted(((i, j) for i in range(4) for j in range(4)), key=lambda p: -HOPS[p[0]] - HOPS[p[1]])[:-1]
FIRST = 0
LINE = [4, 3, 5, 2, 6, 1, 7]


def spot(me):
    return me // 32, (me // 4) % 8, me % 4


def kernel(
    holo_hbm, speed_hbm, weights_hbm, order_hbm, slab_hbm, first_hbm, rowtab_hbm, full_hbm, rest_hbm, wide_hbm,
    out_ref,
    holo, weights, spectral, first, rowtab, full, rest, wide, m1, b1, r1, m2, r2, e1, e2, junk, speed_ref, order_ref, slab_ref,
    load_sem, weight_sem, send_sem, recv_sem, ready,
):
    dist = lax.axis_index("dist")
    me = lax.axis_index("rows")
    barrier = pltpu.get_barrier_semaphore()

    def greet(t):
        pl.semaphore_signal(barrier, inc=1, device_id=(dist, t), device_id_type=MESH)

    loads = [
        pltpu.make_async_copy(source, target, load_sem.at[i])
        for i, (source, target) in enumerate(
            [(holo_hbm, holo), (first_hbm, first), (rowtab_hbm, rowtab), (full_hbm, full), (rest_hbm, rest), (wide_hbm, wide),
             (speed_hbm, speed_ref), (order_hbm, order_ref), (slab_hbm, slab_ref)]
        )
    ]
    for load in loads[:3]:
        load.start()
    y, z, x = spot(me)
    line = [(z + i) % 8 for i in LINE]
    plane = [((y + i) % 4, (x + j) % 4) for i, j in PLANE]
    late = z >= 4
    first_plane = dist == FIRST
    relaxed = jnp.logical_and(first_plane, z < 4)
    telling = jnp.logical_and(first_plane, late)
    for at, to in plane:
        greet(at * 32 + z * 4 + to)
    for at in line:

        @pl.when(jnp.logical_or(jnp.logical_not(telling), at >= 4))
        def _():
            greet(y * 32 + at * 4 + x)

    pl.semaphore_signal(barrier, inc=1, device_id=(1 - dist, me), device_id_type=MESH)
    for load in loads[3:]:
        load.start()
    big = pltpu.make_async_copy(weights_hbm, weights, weight_sem)
    big.start()
    for load in loads[:3]:
        load.wait()
    spectrum = row_stage(holo[...], first[...], rowtab[...])
    for i in range(8):
        for g in range(2):
            m1[2 * i + g] = spectrum[32 * i : 32 * i + 32, 128 * g : 128 * g + 128]

    @pl.when(relaxed)
    def _():
        pl.semaphore_wait(barrier, len(PLANE) + 4)

    @pl.when(jnp.logical_not(relaxed))
    def _():
        pl.semaphore_wait(barrier, len(PLANE) + 8)

    @pl.when(telling)
    def _():
        for at in range(4):
            pl.semaphore_signal(ready, inc=1, device_id=(dist, y * 32 + at * 4 + x), device_id_type=MESH)

    def push(source, target, sent, landed, peer, core=dist):
        pltpu.make_async_remote_copy(
            src_ref=source,
            dst_ref=target,
            send_sem=send_sem.at[sent],
            recv_sem=recv_sem.at[landed],
            device_id=(core, peer),
            device_id_type=MESH,
        ).start()

    def along_line(source, target, landed):
        mine = target.at[pl.ds(2 * z, 2)]
        for at in line:
            push(source.at[pl.ds(2 * at, 2)], mine, 0, landed, y * 32 + at * 4 + x)
        pltpu.make_async_copy(source.at[pl.ds(2 * z, 2)], mine, recv_sem.at[landed]).start()

    def in_plane(source, target, landed):
        def column(at, to):
            return pl.ds(pl.multiple_of(8 * at + 2 * to, 2), 2)

        mine = target.at[:, column(y, x), :]
        for at, to in plane:
            push(source.at[:, column(at, to), :], mine, 2, landed, at * 32 + z * 4 + to)
        pltpu.make_async_copy(source.at[:, column(y, x), :], mine, recv_sem.at[landed]).start()

    def transform(step, carry):
        a, rows = step // 2, pl.ds(pl.multiple_of(step % 2 * 512, 512), 512)
        spectral[a, rows, :] = half(dot(full[rows, :], weights[a]))
        return carry

    @pl.when(first_plane)
    def _():
        in_plane(m1, b1, 0)

    @pl.when(jnp.logical_not(first_plane))
    def _():
        along_line(m1, b1, 0)

    for load in loads[3:]:
        load.wait()
    big.wait()
    lax.fori_loop(0, 4, transform, 0)
    pltpu.make_async_copy(b1, b1, recv_sem.at[0]).wait()

    @pl.when(relaxed)
    def _():
        pl.semaphore_wait(ready, 4)

    @pl.when(first_plane)
    def _():
        along_line(b1, r1, 1)

    @pl.when(jnp.logical_not(first_plane))
    def _():
        in_plane(b1, r1, 1)

    speeds = [speed_ref[i] for i in range(4)]
    filters = filter_stage(dist, me, speeds)
    tf0, tf1, ti0, ti1 = (rest[256 * i : 256 * i + 256, :] for i in range(4))
    ki, perm, kr = rest[1024:1280, :], rest[1280:1536, :], rest[1536:1792, 0:128]
    coltab = wide[...]
    pltpu.make_async_copy(r1, r1, recv_sem.at[1]).wait()
    groups = [jnp.concatenate([r1[2 * i + g] for i in range(8)], axis=0) for g in range(2)]
    inverse = column_stage(groups, tf0, tf1, kr, ki, ti0, ti1, coltab, filters)
    e1[...] = half(inverse)
    swap = pltpu.make_async_remote_copy(
        src_ref=e1,
        dst_ref=e2,
        send_sem=send_sem.at[3],
        recv_sem=recv_sem.at[3],
        device_id=(1 - dist, me),
        device_id_type=MESH,
    )
    swap.start()
    swap.wait_recv()
    inverse = half(inverse + e2[...].astype(jnp.float32))
    m2[0] = inverse[0:128]
    m2[1] = inverse[128:256]
    mine = r2.at[:, pl.ds(pl.multiple_of(32 * z + 8 * y + 2 * x, 2), 2), :]

    def rows(t):
        return m2.at[:, pl.ds(pl.multiple_of(2 * (t // 2), 2), 2), :]

    def layer(step, carry):
        depth = 4 * dist + step
        for core in (1, 0):
            for at, to in plane:
                t = at * 32 + depth * 4 + to
                push(rows(t), mine, 1, 2, t, core)

            @pl.when(jnp.logical_or(depth != z, dist != core))
            def _():
                t = y * 32 + depth * 4 + x
                push(rows(t), mine, 1, 2, t, core)

        return carry

    lax.fori_loop(0, 4, layer, 0)

    @pl.when(z // 4 == dist)
    def _():
        pltpu.make_async_copy(rows(me), mine, recv_sem.at[2]).start()
        pltpu.make_async_copy(rows(me), junk, send_sem.at[1]).start()

    lax.fori_loop(4, 8, transform, 0)
    pltpu.make_async_copy(r2, r2, recv_sem.at[2]).wait()
    recon = half(last_stage([r2[0], r2[1]], perm, lambda a: spectral[order_ref[0, a]]))
    parity = me % 2
    offset = parity * slab_ref[me - parity]
    count = slab_ref[me]
    slot = lax.broadcasted_iota(jnp.int32, (16, 16), 0)
    source = lax.broadcasted_iota(jnp.int32, (16, 16), 1)
    select = half(((source == offset + slot) & (slot < count)).astype(jnp.float32))
    out_ref[...] = half(dot(select, recon))
    swap.wait_send()
    pltpu.make_async_copy(m1.at[pl.ds(0, 14)], b1.at[pl.ds(0, 14)], send_sem.at[0]).wait()
    pltpu.make_async_copy(b1.at[pl.ds(0, 15)], r1.at[pl.ds(0, 15)], send_sem.at[2]).wait()
    pltpu.make_async_copy(r2, r2, send_sem.at[1]).wait()


def on_device(first, rowtab, full, rest, wide, holograms, propagation, weights, angle_order, slab_rows):
    pixels = weights.shape[2]
    holo = holograms.reshape(64, N)
    anywhere = pl.BlockSpec(memory_space=pl.ANY)
    vmem = pltpu.VMEM
    lo = jnp.bfloat16
    return pl.pallas_call(
        kernel,
        out_shape=pltpu.VMEM((16, pixels), lo),
        in_specs=[anywhere] * 10,
        out_specs=pl.BlockSpec(memory_space=vmem),
        scratch_shapes=[
            vmem(holo.shape, lo),
            vmem(weights.shape, lo),
            vmem(weights.shape, lo),
            vmem(first.shape, lo),
            vmem(rowtab.shape, jnp.float32),
            vmem(full.shape, lo),
            vmem(rest.shape, lo),
            vmem(wide.shape, jnp.float32),
            vmem((16, 32, 128), lo),
            vmem((16, 32, 128), lo),
            vmem((16, 32, 128), lo),
            vmem((2, 128, 128), lo),
            vmem((2, 256, 128), lo),
            vmem((256, 128), lo),
            vmem((256, 128), lo),
            vmem((2, 2, 128), lo),
            pltpu.SMEM(propagation.shape, jnp.float32),
            pltpu.SMEM(angle_order.shape, jnp.int32),
            pltpu.SMEM(slab_rows.shape, jnp.int32),
            pltpu.SemaphoreType.DMA((9,)),
            pltpu.SemaphoreType.DMA,
            pltpu.SemaphoreType.DMA((4,)),
            pltpu.SemaphoreType.DMA((4,)),
            pltpu.SemaphoreType.REGULAR,
        ],
        compiler_params=pltpu.CompilerParams(collective_id=0, has_side_effects=True),
    )(holo, propagation, weights, angle_order, slab_rows, first, rowtab, full, rest, wide)


def solution(mesh):
    constants = tables()

    def whole(*args):
        return jax.shard_map(
            on_device,
            mesh=mesh,
            in_specs=(P(),) * 5
            + (P(None, None, "dist", "rows"), P(), P(None, None, "dist"), P(), P()),
            out_specs=P("rows", "dist"),
            check_vma=False,
        )(*(jnp.asarray(c) for c in constants), *args)

    return whole
```

```python
import math

import jax
import jax.numpy as jnp
import numpy as np
from jax import lax
from jax.experimental import pallas as pl
from jax.experimental.pallas import tpu as pltpu
from jax.sharding import PartitionSpec as P

absorb_ratio = 0.1
regularizer = 0.05
MESH = pl.DeviceIdType.MESH
N = 1024
ROWS = 128
ROOT = 1.0 / 32.0
RADIX = 8


def tables():
    long = np.arange(ROWS)
    short = np.arange(RADIX)
    turn = 2.0 * math.pi
    beta = turn * (np.outer(long, long) % ROWS) / ROWS
    cas = [np.cos(beta) + np.sin(beta), np.cos(beta) - np.sin(beta)]
    eye2 = np.eye(2)
    ts, tf, ti = [], [], []
    place = long.reshape(4, 8, 4).transpose(1, 0, 2).reshape(-1)
    for c in cas:
        ts.append(np.einsum("tk,bc->tbck", c[place], eye2).reshape(256, 256))
        tf.append(ts[-1].T)
        ti.append(np.einsum("jpk,bc->pjbck", c.reshape(64, 2, ROWS), eye2).reshape(256, 256))
    phi = turn * (np.outer(short, short) % RADIX) / RADIX
    wave = [np.cos(phi), np.sin(phi)]
    kr = np.concatenate([np.kron(np.eye(16), w) for w in wave], axis=0)
    ki = np.stack([np.einsum("ij,ab,d,my->iadmjby", np.eye(4), np.eye(4), np.ones(2), w) for w in wave])
    ki = np.moveaxis(ki, 0, 4).reshape(256, 256)
    spectral = (8 * place[None, :, None] + (2 * short[:4, None, None] + short[None, None, :2])).reshape(-1)
    angle = turn * (np.outer(spectral, np.arange(N)) % N) / N
    full = (np.cos(angle) + np.sin(angle)) * ROOT
    theta = turn * np.outer(short, long) / N
    rowtab = np.concatenate([np.cos(theta), np.sin(theta)], axis=0) * ROOT
    tk = theta.T[:, np.arange(128) % RADIX]
    coltab = np.concatenate([np.cos(tk), np.sin(tk)], axis=0) * ROOT
    first = np.concatenate(ts, axis=1)
    rest = np.concatenate(tf + ti + [ki, np.pad(kr, ((0, 0), (0, 128)))], axis=0)
    half = lambda v: np.asarray(v, np.float32).astype(jnp.bfloat16)
    return half(first), rowtab.astype(np.float32), half(full), half(rest), coltab.astype(np.float32)


def dot(a, b):
    return jnp.dot(a, b, preferred_element_type=jnp.float32)


def half(value):
    return value.astype(jnp.bfloat16)


def row_stage(holo, first, rowtab):
    h = [holo[:, 128 * i : 128 * (i + 1)].astype(jnp.float32) for i in range(RADIX)]
    e = [h[i] + h[i + 4] for i in range(4)]
    o = [h[i] - h[i + 4] for i in range(4)]
    c = math.sqrt(0.5)
    even, odd = e[0] + e[2], e[1] + e[3]
    minus, plus = c * (o[1] - o[3]), c * (o[1] + o[3])
    p0, p4 = even + odd, even - odd
    p2, q2 = e[0] - e[2], e[1] - e[3]
    p1, q1 = o[0] + minus, o[2] + plus
    p3, q3 = o[0] - minus, plus - o[2]
    parts = [(p0, None), (p1, q1), (p2, q2), (p3, q3), (p4, None), (p3, -q3), (p2, -q2), (p1, -q1)]
    straight, turned = [], []
    for j, (p, q) in enumerate(parts):
        cos, sin = rowtab[j : j + 1, :], rowtab[RADIX + j : RADIX + j + 1, :]
        if q is None:
            straight.append(half(cos * p))
            turned.append(half(sin * p))
        else:
            straight.append(half(cos * p - sin * q))
            turned.append(half(sin * p + cos * q))
    blocks = [
        jnp.concatenate([straight[2 * i], straight[2 * i + 1], turned[2 * i], turned[2 * i + 1]], axis=1)
        for i in range(4)
    ]
    rhs = jnp.concatenate(blocks, axis=0)
    out = lax.dot_general(first, rhs, (((1,), (1,)), ((), ())), preferred_element_type=jnp.float32)
    return half(out)


def sine(x):
    n = jnp.floor(x * (1.0 / math.pi) + 0.5)
    r = x - n * 3.140625
    r = r - n * 9.67502593994140625e-4
    r = r - n * 1.509957990978376432e-7
    s = r * r
    w = -2.5052108385441718775e-8
    for coefficient in (
        2.7557319223985890653e-6,
        -1.9841269841269841253e-4,
        8.3333333333333332177e-3,
        -1.6666666666666665741e-1,
    ):
        w = w * s + coefficient
    value = r + r * s * w
    return jnp.where(n - 2.0 * jnp.floor(n * 0.5) > 0.5, -value, value)


def roll(value, shift):
    return pltpu.roll(value, shift % 128, 1)


def filter_stage(dist, me, speeds, roll=roll):
    lane = lax.broadcasted_iota(jnp.int32, (1, 128), 1)
    m = lane % 8
    second = (lane // 8) % 2 == 1
    odd_angle = (lane // 16) % 2 == 1
    other = odd_angle != (dist == 1)
    speed = jnp.where(
        other,
        jnp.where(second, speeds[3], speeds[2]),
        jnp.where(second, speeds[1], speeds[0]),
    )
    k = lax.broadcasted_iota(jnp.int32, (128, 128), 0)
    ky = k + 128 * m
    ky = jnp.where(ky < 512, ky, ky - 1024).astype(jnp.float32)
    ky2 = ky * ky
    shift = math.atan(absorb_ratio)
    gain = 2.0 * math.sqrt(1.0 + absorb_ratio * absorb_ratio)
    result = []
    for g in range(2):
        blocks = []
        for b in range(2):
            kx = 8 * me + 4 * g + 2 * (lane // 64) + b
            kx = jnp.where(kx < 512, kx, kx - 1024).astype(jnp.float32)
            radius = (ky2 + kx * kx) * (1.0 / (N * N))
            t = gain * sine(speed * radius + shift)
            total = t * t
            total = total + jnp.where(second, roll(total, 8), roll(total, -8))
            total = total + jnp.where(odd_angle, roll(total, 16), roll(total, -16))
            f = t / (total + regularizer)
            blocks.append(jnp.where(odd_angle, roll(f, 16), f))
        result.append(jnp.concatenate(blocks, axis=0))
    return result


def twist(cos, sin, u, v):
    return cos * u + sin * v, cos * v - sin * u


def twice(table):
    return jnp.concatenate([table, table], axis=0)


def column_stage(groups, tf0, tf1, kr, ki, ti0, ti1, coltab, filters):
    cos, sin = twice(coltab[0:128]), twice(coltab[128:256])
    r = jnp.concatenate(groups, axis=1)
    u, v = dot(tf0, r), dot(tf1, r)
    numer = []
    for g in range(2):
        part = slice(128 * g, 128 * g + 128)
        x, y = twist(cos, sin, u[:, part], v[:, part])
        spec = dot(jnp.concatenate([half(x), half(y)], axis=1), kr)
        numer.append(half(spec * filters[g]))
    pq = dot(jnp.concatenate(numer, axis=1), ki)
    p, q = pq[:, 0:128], pq[:, 128:256]
    straight = half(cos * p - sin * q)
    turned = half(sin * p + cos * q)
    return dot(ti0, straight) + dot(ti1, turned)


def last_stage(pair, weight_of):
    turned = [r.astype(jnp.float32).T for r in pair]
    total = None
    for a in range(4):
        tiles = []
        for j in range(4):
            at = (j * 4 + a) * 8
            tiles.append(jnp.concatenate([half_turned[at : at + 8, :] for half_turned in turned], axis=0))
        term = dot(half(jnp.concatenate(tiles, axis=1)), weight_of(a))
        total = term if total is None else total + term
    return total


HOPS = [0, 1, 2, 1]
PLANE = sorted(((i, j) for i in range(4) for j in range(4)), key=lambda p: -HOPS[p[0]] - HOPS[p[1]])[:-1]
FIRST = 0
LINE = [4, 3, 5, 2, 6, 1, 7]


def spot(me):
    return me // 32, (me // 4) % 8, me % 4


def kernel(
    holo_hbm, speed_hbm, weights_hbm, order_hbm, slab_hbm, first_hbm, rowtab_hbm, full_hbm, rest_hbm, wide_hbm,
    out_ref,
    holo, weights, spectral, first, rowtab, full, rest, wide, m1, b1, r1, m2, r2, e1, e2, junk, speed_ref, order_ref, slab_ref,
    load_sem, weight_sem, send_sem, recv_sem, ready,
):
    dist = lax.axis_index("dist")
    me = lax.axis_index("rows")
    barrier = pltpu.get_barrier_semaphore()

    def greet(t):
        pl.semaphore_signal(barrier, inc=1, device_id=(dist, t), device_id_type=MESH)

    loads = [
        pltpu.make_async_copy(source, target, load_sem.at[i])
        for i, (source, target) in enumerate(
            [(holo_hbm, holo), (first_hbm, first), (rowtab_hbm, rowtab), (full_hbm, full), (rest_hbm, rest), (wide_hbm, wide),
             (speed_hbm, speed_ref), (order_hbm, order_ref), (slab_hbm, slab_ref)]
        )
    ]
    for load in loads[:3]:
        load.start()
    y, z, x = spot(me)
    line = [(z + i) % 8 for i in LINE]
    plane = [((y + i) % 4, (x + j) % 4) for i, j in PLANE]
    late = z >= 4
    first_plane = dist == FIRST
    relaxed = jnp.logical_and(first_plane, z < 4)
    telling = jnp.logical_and(first_plane, late)
    for at, to in plane:
        greet(at * 32 + z * 4 + to)
    for at in line:

        @pl.when(jnp.logical_or(jnp.logical_not(telling), at >= 4))
        def _():
            greet(y * 32 + at * 4 + x)

    pl.semaphore_signal(barrier, inc=1, device_id=(1 - dist, me), device_id_type=MESH)
    for load in loads[3:]:
        load.start()
    big = pltpu.make_async_copy(weights_hbm, weights, weight_sem)
    big.start()
    for load in loads[:3]:
        load.wait()
    spectrum = row_stage(holo[...], first[...], rowtab[...])
    for i in range(8):
        for g in range(2):
            m1[2 * i + g] = spectrum[32 * i : 32 * i + 32, 128 * g : 128 * g + 128]

    @pl.when(relaxed)
    def _():
        pl.semaphore_wait(barrier, len(PLANE) + 4)

    @pl.when(jnp.logical_not(relaxed))
    def _():
        pl.semaphore_wait(barrier, len(PLANE) + 8)

    @pl.when(telling)
    def _():
        for at in range(4):
            pl.semaphore_signal(ready, inc=1, device_id=(dist, y * 32 + at * 4 + x), device_id_type=MESH)

    def push(source, target, sent, landed, peer, core=dist):
        pltpu.make_async_remote_copy(
            src_ref=source,
            dst_ref=target,
            send_sem=send_sem.at[sent],
            recv_sem=recv_sem.at[landed],
            device_id=(core, peer),
            device_id_type=MESH,
        ).start()

    def along_line(source, target, landed):
        mine = target.at[pl.ds(2 * z, 2)]
        for at in line:
            push(source.at[pl.ds(2 * at, 2)], mine, 0, landed, y * 32 + at * 4 + x)
        pltpu.make_async_copy(source.at[pl.ds(2 * z, 2)], mine, recv_sem.at[landed]).start()

    def in_plane(source, target, landed):
        def column(at, to):
            return pl.ds(pl.multiple_of(8 * at + 2 * to, 2), 2)

        mine = target.at[:, column(y, x), :]
        for at, to in plane:
            push(source.at[:, column(at, to), :], mine, 2, landed, at * 32 + z * 4 + to)
        pltpu.make_async_copy(source.at[:, column(y, x), :], mine, recv_sem.at[landed]).start()

    def transform(step, carry):
        a, rows = step // 2, pl.ds(pl.multiple_of(step % 2 * 512, 512), 512)
        spectral[a, rows, :] = half(dot(full[rows, :], weights[a]))
        return carry

    @pl.when(first_plane)
    def _():
        in_plane(m1, b1, 0)

    @pl.when(jnp.logical_not(first_plane))
    def _():
        along_line(m1, b1, 0)

    for load in loads[3:]:
        load.wait()
    big.wait()
    lax.fori_loop(0, 4, transform, 0)
    pltpu.make_async_copy(b1, b1, recv_sem.at[0]).wait()

    @pl.when(relaxed)
    def _():
        pl.semaphore_wait(ready, 4)

    @pl.when(first_plane)
    def _():
        along_line(b1, r1, 1)

    @pl.when(jnp.logical_not(first_plane))
    def _():
        in_plane(b1, r1, 1)

    speeds = [speed_ref[i] for i in range(4)]
    filters = filter_stage(dist, me, speeds)
    tf0, tf1, ti0, ti1 = (rest[256 * i : 256 * i + 256, :] for i in range(4))
    ki, kr = rest[1024:1280, :], rest[1280:1536, 0:128]
    coltab = wide[...]
    pltpu.make_async_copy(r1, r1, recv_sem.at[1]).wait()
    groups = [jnp.concatenate([r1[2 * i + g] for i in range(8)], axis=0) for g in range(2)]
    inverse = column_stage(groups, tf0, tf1, kr, ki, ti0, ti1, coltab, filters)
    e1[...] = half(inverse)
    swap = pltpu.make_async_remote_copy(
        src_ref=e1,
        dst_ref=e2,
        send_sem=send_sem.at[3],
        recv_sem=recv_sem.at[3],
        device_id=(1 - dist, me),
        device_id_type=MESH,
    )
    swap.start()
    swap.wait_recv()
    inverse = half(inverse + e2[...].astype(jnp.float32))
    m2[0] = inverse[0:128]
    m2[1] = inverse[128:256]
    mine = r2.at[:, pl.ds(pl.multiple_of(32 * z + 8 * y + 2 * x, 2), 2), :]

    def rows(t):
        return m2.at[:, pl.ds(pl.multiple_of(2 * (t // 2), 2), 2), :]

    def layer(step, carry):
        depth = 4 * dist + step
        for core in (1, 0):
            for at, to in plane:
                t = at * 32 + depth * 4 + to
                push(rows(t), mine, 1, 2, t, core)

            @pl.when(jnp.logical_or(depth != z, dist != core))
            def _():
                t = y * 32 + depth * 4 + x
                push(rows(t), mine, 1, 2, t, core)

        return carry

    lax.fori_loop(0, 4, layer, 0)

    @pl.when(z // 4 == dist)
    def _():
        pltpu.make_async_copy(rows(me), mine, recv_sem.at[2]).start()
        pltpu.make_async_copy(rows(me), junk, send_sem.at[1]).start()

    lax.fori_loop(4, 8, transform, 0)
    pltpu.make_async_copy(r2, r2, recv_sem.at[2]).wait()
    recon = half(last_stage([r2[0], r2[1]], lambda a: spectral[order_ref[0, a]]))
    parity = me % 2
    offset = parity * slab_ref[me - parity]
    count = slab_ref[me]
    slot = lax.broadcasted_iota(jnp.int32, (16, 16), 0)
    source = lax.broadcasted_iota(jnp.int32, (16, 16), 1)
    select = half(((source == offset + slot) & (slot < count)).astype(jnp.float32))
    out_ref[...] = half(dot(select, recon))
    swap.wait_send()
    pltpu.make_async_copy(m1.at[pl.ds(0, 14)], b1.at[pl.ds(0, 14)], send_sem.at[0]).wait()
    pltpu.make_async_copy(b1.at[pl.ds(0, 15)], r1.at[pl.ds(0, 15)], send_sem.at[2]).wait()
    pltpu.make_async_copy(r2, r2, send_sem.at[1]).wait()


def on_device(first, rowtab, full, rest, wide, holograms, propagation, weights, angle_order, slab_rows):
    pixels = weights.shape[2]
    holo = holograms.reshape(64, N)
    anywhere = pl.BlockSpec(memory_space=pl.ANY)
    vmem = pltpu.VMEM
    lo = jnp.bfloat16
    return pl.pallas_call(
        kernel,
        out_shape=pltpu.VMEM((16, pixels), lo),
        in_specs=[anywhere] * 10,
        out_specs=pl.BlockSpec(memory_space=vmem),
        scratch_shapes=[
            vmem(holo.shape, lo),
            vmem(weights.shape, lo),
            vmem(weights.shape, lo),
            vmem(first.shape, lo),
            vmem(rowtab.shape, jnp.float32),
            vmem(full.shape, lo),
            vmem(rest.shape, lo),
            vmem(wide.shape, jnp.float32),
            vmem((16, 32, 128), lo),
            vmem((16, 32, 128), lo),
            vmem((16, 32, 128), lo),
            vmem((2, 128, 128), lo),
            vmem((2, 256, 128), lo),
            vmem((256, 128), lo),
            vmem((256, 128), lo),
            vmem((2, 2, 128), lo),
            pltpu.SMEM(propagation.shape, jnp.float32),
            pltpu.SMEM(angle_order.shape, jnp.int32),
            pltpu.SMEM(slab_rows.shape, jnp.int32),
            pltpu.SemaphoreType.DMA((9,)),
            pltpu.SemaphoreType.DMA,
            pltpu.SemaphoreType.DMA((4,)),
            pltpu.SemaphoreType.DMA((4,)),
            pltpu.SemaphoreType.REGULAR,
        ],
        compiler_params=pltpu.CompilerParams(collective_id=0, has_side_effects=True),
    )(holo, propagation, weights, angle_order, slab_rows, first, rowtab, full, rest, wide)


def solution(mesh):
    constants = tables()

    def whole(*args):
        return jax.shard_map(
            on_device,
            mesh=mesh,
            in_specs=(P(),) * 5
            + (P(None, None, "dist", "rows"), P(), P(None, None, "dist"), P(), P()),
            out_specs=P("rows", "dist"),
            check_vma=False,
        )(*(jnp.asarray(c) for c in constants), *args)

    return whole
```

```python
import math

import jax
import jax.numpy as jnp
import numpy as np
from jax import lax
from jax.experimental import pallas as pl
from jax.experimental.pallas import tpu as pltpu
from jax.sharding import PartitionSpec as P

absorb_ratio = 0.1
regularizer = 0.05
MESH = pl.DeviceIdType.MESH
N = 1024
ROWS = 128
ROOT = 1.0 / 32.0
RADIX = 8


def tables():
    long = np.arange(ROWS)
    short = np.arange(RADIX)
    turn = 2.0 * math.pi
    beta = turn * (np.outer(long, long) % ROWS) / ROWS
    cas = [np.cos(beta) + np.sin(beta), np.cos(beta) - np.sin(beta)]
    eye2 = np.eye(2)
    ts, tf, ti = [], [], []
    place = long.reshape(4, 8, 4).transpose(1, 0, 2).reshape(-1)
    for c in cas:
        ts.append(np.einsum("tk,bc->tbck", c[place], eye2).reshape(256, 256))
        tf.append(ts[-1].T)
        ti.append(np.einsum("jpk,bc->pjbck", c.reshape(64, 2, ROWS), eye2).reshape(256, 256))
    phi = turn * (np.outer(short, short) % RADIX) / RADIX
    wave = [np.cos(phi), np.sin(phi)]
    kr = np.concatenate([np.kron(np.eye(16), w) for w in wave], axis=0)
    ki = np.stack([np.einsum("ij,ab,d,my->iadmjby", np.eye(4), np.eye(4), np.ones(2), w) for w in wave])
    ki = np.moveaxis(ki, 0, 4).reshape(256, 256)
    spectral = (8 * place[None, :, None] + (2 * short[:4, None, None] + short[None, None, :2])).reshape(-1)
    angle = turn * (np.outer(spectral, np.arange(N)) % N) / N
    full = (np.cos(angle) + np.sin(angle)) * ROOT
    theta = turn * np.outer(short, long) / N
    rowtab = np.concatenate([np.cos(theta), np.sin(theta)], axis=0) * ROOT
    tk = theta.T[:, np.arange(128) % RADIX]
    coltab = np.concatenate([np.cos(tk), np.sin(tk)], axis=0) * ROOT
    first = np.concatenate(ts, axis=1)
    rest = np.concatenate(tf + ti + [ki, np.pad(kr, ((0, 0), (0, 128)))], axis=0)
    half = lambda v: np.asarray(v, np.float32).astype(jnp.bfloat16)
    return half(first), rowtab.astype(np.float32), half(full), half(rest), coltab.astype(np.float32)


def dot(a, b):
    return jnp.dot(a, b, preferred_element_type=jnp.float32)


def half(value):
    return value.astype(jnp.bfloat16)


def row_stage(holo, first, rowtab):
    h = [holo[:, 128 * i : 128 * (i + 1)].astype(jnp.float32) for i in range(RADIX)]
    e = [h[i] + h[i + 4] for i in range(4)]
    o = [h[i] - h[i + 4] for i in range(4)]
    c = math.sqrt(0.5)
    even, odd = e[0] + e[2], e[1] + e[3]
    minus, plus = c * (o[1] - o[3]), c * (o[1] + o[3])
    p0, p4 = even + odd, even - odd
    p2, q2 = e[0] - e[2], e[1] - e[3]
    p1, q1 = o[0] + minus, o[2] + plus
    p3, q3 = o[0] - minus, plus - o[2]
    parts = [(p0, None), (p1, q1), (p2, q2), (p3, q3), (p4, None), (p3, -q3), (p2, -q2), (p1, -q1)]
    straight, turned = [], []
    for j, (p, q) in enumerate(parts):
        cos, sin = rowtab[j : j + 1, :], rowtab[RADIX + j : RADIX + j + 1, :]
        if q is None:
            straight.append(half(cos * p))
            turned.append(half(sin * p))
        else:
            straight.append(half(cos * p - sin * q))
            turned.append(half(sin * p + cos * q))
    blocks = [
        jnp.concatenate([straight[2 * i], straight[2 * i + 1], turned[2 * i], turned[2 * i + 1]], axis=1)
        for i in range(4)
    ]
    rhs = jnp.concatenate(blocks, axis=0)
    out = lax.dot_general(first, rhs, (((1,), (1,)), ((), ())), preferred_element_type=jnp.float32)
    return half(out)


def sine(x):
    n = jnp.floor(x * (1.0 / math.pi) + 0.5)
    r = x - n * 3.140625
    r = r - n * 9.67502593994140625e-4
    r = r - n * 1.509957990978376432e-7
    s = r * r
    w = -2.5052108385441718775e-8
    for coefficient in (
        2.7557319223985890653e-6,
        -1.9841269841269841253e-4,
        8.3333333333333332177e-3,
        -1.6666666666666665741e-1,
    ):
        w = w * s + coefficient
    value = r + r * s * w
    return jnp.where(n - 2.0 * jnp.floor(n * 0.5) > 0.5, -value, value)


def roll(value, shift):
    return pltpu.roll(value, shift % 128, 1)


def filter_stage(dist, me, speeds, roll=roll):
    lane = lax.broadcasted_iota(jnp.int32, (1, 128), 1)
    m = lane % 8
    second = (lane // 8) % 2 == 1
    odd_angle = (lane // 16) % 2 == 1
    other = odd_angle != (dist == 1)
    speed = jnp.where(
        other,
        jnp.where(second, speeds[3], speeds[2]),
        jnp.where(second, speeds[1], speeds[0]),
    )
    k = lax.broadcasted_iota(jnp.int32, (128, 128), 0)
    ky = k + 128 * m
    ky = jnp.where(ky < 512, ky, ky - 1024).astype(jnp.float32)
    ky2 = ky * ky
    shift = math.atan(absorb_ratio)
    gain = 2.0 * math.sqrt(1.0 + absorb_ratio * absorb_ratio)
    result = []
    for g in range(2):
        blocks = []
        for b in range(2):
            kx = 8 * me + 4 * g + 2 * (lane // 64) + b
            kx = jnp.where(kx < 512, kx, kx - 1024).astype(jnp.float32)
            radius = (ky2 + kx * kx) * (1.0 / (N * N))
            t = gain * sine(speed * radius + shift)
            total = t * t
            total = total + jnp.where(second, roll(total, 8), roll(total, -8))
            total = total + jnp.where(odd_angle, roll(total, 16), roll(total, -16))
            f = t / (total + regularizer)
            blocks.append(jnp.where(odd_angle, roll(f, 16), f))
        result.append(jnp.concatenate(blocks, axis=0))
    return result


def twist(cos, sin, u, v):
    return cos * u + sin * v, cos * v - sin * u


def twice(table):
    return jnp.concatenate([table, table], axis=0)


def column_stage(groups, tf, kr, ki, ti0, ti1, coltab, filters):
    cos, sin = twice(coltab[0:128]), twice(coltab[128:256])
    r = jnp.concatenate(groups, axis=1)
    both = dot(tf, r)
    u, v = both[0:256], both[256:512]
    numer = []
    for g in range(2):
        part = slice(128 * g, 128 * g + 128)
        x, y = twist(cos, sin, u[:, part], v[:, part])
        spec = dot(jnp.concatenate([half(x), half(y)], axis=1), kr)
        numer.append(half(spec * filters[g]))
    pq = dot(jnp.concatenate(numer, axis=1), ki)
    p, q = pq[:, 0:128], pq[:, 128:256]
    straight = half(cos * p - sin * q)
    turned = half(sin * p + cos * q)
    return dot(ti0, straight) + dot(ti1, turned)


def last_stage(pair, weight_of):
    turned = [r.astype(jnp.float32).T for r in pair]
    total = None
    for a in range(4):
        tiles = []
        for j in range(4):
            at = (j * 4 + a) * 8
            tiles.append(jnp.concatenate([half_turned[at : at + 8, :] for half_turned in turned], axis=0))
        term = dot(half(jnp.concatenate(tiles, axis=1)), weight_of(a))
        total = term if total is None else total + term
    return total


HOPS = [0, 1, 2, 1]
PLANE = sorted(((i, j) for i in range(4) for j in range(4)), key=lambda p: -HOPS[p[0]] - HOPS[p[1]])[:-1]
FIRST = 0
LINE = [4, 3, 5, 2, 6, 1, 7]


def spot(me):
    return me // 32, (me // 4) % 8, me % 4


def kernel(
    holo_hbm, speed_hbm, weights_hbm, order_hbm, slab_hbm, first_hbm, rowtab_hbm, full_hbm, rest_hbm, wide_hbm,
    out_ref,
    holo, weights, spectral, first, rowtab, full, rest, wide, m1, b1, r1, m2, r2, e1, e2, junk, speed_ref, order_ref, slab_ref,
    load_sem, weight_sem, send_sem, recv_sem, ready,
):
    dist = lax.axis_index("dist")
    me = lax.axis_index("rows")
    barrier = pltpu.get_barrier_semaphore()

    def greet(t):
        pl.semaphore_signal(barrier, inc=1, device_id=(dist, t), device_id_type=MESH)

    loads = [
        pltpu.make_async_copy(source, target, load_sem.at[i])
        for i, (source, target) in enumerate(
            [(holo_hbm, holo), (first_hbm, first), (rowtab_hbm, rowtab), (full_hbm, full), (rest_hbm, rest), (wide_hbm, wide),
             (speed_hbm, speed_ref), (order_hbm, order_ref), (slab_hbm, slab_ref)]
        )
    ]
    for load in loads[:3]:
        load.start()
    y, z, x = spot(me)
    line = [(z + i) % 8 for i in LINE]
    plane = [((y + i) % 4, (x + j) % 4) for i, j in PLANE]
    late = z >= 4
    first_plane = dist == FIRST
    relaxed = jnp.logical_and(first_plane, z < 4)
    telling = jnp.logical_and(first_plane, late)
    for at, to in plane:
        greet(at * 32 + z * 4 + to)
    for at in line:

        @pl.when(jnp.logical_or(jnp.logical_not(telling), at >= 4))
        def _():
            greet(y * 32 + at * 4 + x)

    pl.semaphore_signal(barrier, inc=1, device_id=(1 - dist, me), device_id_type=MESH)
    for load in loads[3:]:
        load.start()
    big = pltpu.make_async_copy(weights_hbm, weights, weight_sem)
    big.start()
    for load in loads[:3]:
        load.wait()
    spectrum = row_stage(holo[...], first[...], rowtab[...])
    for i in range(8):
        for g in range(2):
            m1[2 * i + g] = spectrum[32 * i : 32 * i + 32, 128 * g : 128 * g + 128]

    @pl.when(relaxed)
    def _():
        pl.semaphore_wait(barrier, len(PLANE) + 4)

    @pl.when(jnp.logical_not(relaxed))
    def _():
        pl.semaphore_wait(barrier, len(PLANE) + 8)

    @pl.when(telling)
    def _():
        for at in range(4):
            pl.semaphore_signal(ready, inc=1, device_id=(dist, y * 32 + at * 4 + x), device_id_type=MESH)

    def push(source, target, sent, landed, peer, core=dist):
        pltpu.make_async_remote_copy(
            src_ref=source,
            dst_ref=target,
            send_sem=send_sem.at[sent],
            recv_sem=recv_sem.at[landed],
            device_id=(core, peer),
            device_id_type=MESH,
        ).start()

    def along_line(source, target, landed):
        mine = target.at[pl.ds(2 * z, 2)]
        for at in line:
            push(source.at[pl.ds(2 * at, 2)], mine, 0, landed, y * 32 + at * 4 + x)
        pltpu.make_async_copy(source.at[pl.ds(2 * z, 2)], mine, recv_sem.at[landed]).start()

    def in_plane(source, target, landed):
        def column(at, to):
            return pl.ds(pl.multiple_of(8 * at + 2 * to, 2), 2)

        mine = target.at[:, column(y, x), :]
        for at, to in plane:
            push(source.at[:, column(at, to), :], mine, 2, landed, at * 32 + z * 4 + to)
        pltpu.make_async_copy(source.at[:, column(y, x), :], mine, recv_sem.at[landed]).start()

    def transform(step, carry):
        a, rows = step // 2, pl.ds(pl.multiple_of(step % 2 * 512, 512), 512)
        spectral[a, rows, :] = half(dot(full[rows, :], weights[a]))
        return carry

    @pl.when(first_plane)
    def _():
        in_plane(m1, b1, 0)

    @pl.when(jnp.logical_not(first_plane))
    def _():
        along_line(m1, b1, 0)

    for load in loads[3:]:
        load.wait()
    big.wait()
    lax.fori_loop(0, 4, transform, 0)
    pltpu.make_async_copy(b1, b1, recv_sem.at[0]).wait()

    @pl.when(relaxed)
    def _():
        pl.semaphore_wait(ready, 4)

    @pl.when(first_plane)
    def _():
        along_line(b1, r1, 1)

    @pl.when(jnp.logical_not(first_plane))
    def _():
        in_plane(b1, r1, 1)

    speeds = [speed_ref[i] for i in range(4)]
    filters = filter_stage(dist, me, speeds)
    tf, ti0, ti1 = rest[0:512, :], rest[512:768, :], rest[768:1024, :]
    ki, kr = rest[1024:1280, :], rest[1280:1536, 0:128]
    coltab = wide[...]
    pltpu.make_async_copy(r1, r1, recv_sem.at[1]).wait()
    groups = [jnp.concatenate([r1[2 * i + g] for i in range(8)], axis=0) for g in range(2)]
    inverse = column_stage(groups, tf, kr, ki, ti0, ti1, coltab, filters)
    e1[...] = half(inverse)
    swap = pltpu.make_async_remote_copy(
        src_ref=e1,
        dst_ref=e2,
        send_sem=send_sem.at[3],
        recv_sem=recv_sem.at[3],
        device_id=(1 - dist, me),
        device_id_type=MESH,
    )
    swap.start()
    swap.wait_recv()
    inverse = half(inverse + e2[...].astype(jnp.float32))
    m2[0] = inverse[0:128]
    m2[1] = inverse[128:256]
    mine = r2.at[:, pl.ds(pl.multiple_of(32 * z + 8 * y + 2 * x, 2), 2), :]

    def rows(t):
        return m2.at[:, pl.ds(pl.multiple_of(2 * (t // 2), 2), 2), :]

    def layer(step, carry):
        depth = 4 * dist + step
        for core in (1, 0):
            for at, to in plane:
                t = at * 32 + depth * 4 + to
                push(rows(t), mine, 1, 2, t, core)

            @pl.when(jnp.logical_or(depth != z, dist != core))
            def _():
                t = y * 32 + depth * 4 + x
                push(rows(t), mine, 1, 2, t, core)

        return carry

    lax.fori_loop(0, 4, layer, 0)

    @pl.when(z // 4 == dist)
    def _():
        pltpu.make_async_copy(rows(me), mine, recv_sem.at[2]).start()
        pltpu.make_async_copy(rows(me), junk, send_sem.at[1]).start()

    lax.fori_loop(4, 8, transform, 0)
    parity = me % 2
    offset = parity * slab_ref[me - parity]
    count = slab_ref[me]
    slot = lax.broadcasted_iota(jnp.int32, (16, 16), 0)
    source = lax.broadcasted_iota(jnp.int32, (16, 16), 1)
    select = half(((source == offset + slot) & (slot < count)).astype(jnp.float32))
    orders = [order_ref[0, a] for a in range(4)]
    pltpu.make_async_copy(r2, r2, recv_sem.at[2]).wait()
    recon = half(last_stage([r2[0], r2[1]], lambda a: spectral[orders[a]]))
    out_ref[...] = half(dot(select, recon))
    swap.wait_send()
    pltpu.make_async_copy(m1.at[pl.ds(0, 14)], b1.at[pl.ds(0, 14)], send_sem.at[0]).wait()
    pltpu.make_async_copy(b1.at[pl.ds(0, 15)], r1.at[pl.ds(0, 15)], send_sem.at[2]).wait()
    pltpu.make_async_copy(r2, r2, send_sem.at[1]).wait()


def on_device(first, rowtab, full, rest, wide, holograms, propagation, weights, angle_order, slab_rows):
    pixels = weights.shape[2]
    holo = holograms.reshape(64, N)
    anywhere = pl.BlockSpec(memory_space=pl.ANY)
    vmem = pltpu.VMEM
    lo = jnp.bfloat16
    return pl.pallas_call(
        kernel,
        out_shape=pltpu.VMEM((16, pixels), lo),
        in_specs=[anywhere] * 10,
        out_specs=pl.BlockSpec(memory_space=vmem),
        scratch_shapes=[
            vmem(holo.shape, lo),
            vmem(weights.shape, lo),
            vmem(weights.shape, lo),
            vmem(first.shape, lo),
            vmem(rowtab.shape, jnp.float32),
            vmem(full.shape, lo),
            vmem(rest.shape, lo),
            vmem(wide.shape, jnp.float32),
            vmem((16, 32, 128), lo),
            vmem((16, 32, 128), lo),
            vmem((16, 32, 128), lo),
            vmem((2, 128, 128), lo),
            vmem((2, 256, 128), lo),
            vmem((256, 128), lo),
            vmem((256, 128), lo),
            vmem((2, 2, 128), lo),
            pltpu.SMEM(propagation.shape, jnp.float32),
            pltpu.SMEM(angle_order.shape, jnp.int32),
            pltpu.SMEM(slab_rows.shape, jnp.int32),
            pltpu.SemaphoreType.DMA((9,)),
            pltpu.SemaphoreType.DMA,
            pltpu.SemaphoreType.DMA((4,)),
            pltpu.SemaphoreType.DMA((4,)),
            pltpu.SemaphoreType.REGULAR,
        ],
        compiler_params=pltpu.CompilerParams(collective_id=0, has_side_effects=True),
    )(holo, propagation, weights, angle_order, slab_rows, first, rowtab, full, rest, wide)


def solution(mesh):
    constants = tables()

    def whole(*args):
        return jax.shard_map(
            on_device,
            mesh=mesh,
            in_specs=(P(),) * 5
            + (P(None, None, "dist", "rows"), P(), P(None, None, "dist"), P(), P()),
            out_specs=P("rows", "dist"),
            check_vma=False,
        )(*(jnp.asarray(c) for c in constants), *args)

    return whole
```
